512 devices in a mesh: mesh: 32 (over y, z_lo), panel: 16 (over z_hi, x, core).
Axes of the slice: x: 4, y: 8, z: 8 (z_hi: 2, z_lo: 4; z = z_hi * 4 + z_lo), core: 2. Of those that a mesh axis runs over, the one named last changes fastest.
Arguments:
- basis_vectors: bfloat16 [256, 1024, 192], P('mesh', 'panel'), may hold values from -0.75 to 0.75
- stiffness_blocks: bfloat16 [1792, 192, 192], P('mesh'), may hold values from -0.21875 to 0.21875
- block_rows: int32 [1792], P('mesh'), may hold values from 0 to 7
- block_columns: int32 [1792], P('mesh'), may hold values from 0 to 23
- density: float32 [1792], P('mesh'), may hold values from 0.1 to 1
- block_counts: int32 [32], P('mesh'), may hold values from 14 to 56, as said below
- send_list: int32 [512], P('mesh'), may hold values from 0 to 7
Outputs:
- reduced: float32 [1024, 1024], P('panel', 'mesh')
The draws below stay inside these ranges and needn't reach their ends.
Inputs may be any that keep to these rules, and one draw needn't show every extreme that they name: `block_counts`: in every draw some partition holds exactly 56 and another exactly 14.
All inputs are finite; a program needn't handle non-finite values.
Results may differ from the reference program's by a relative error of at most 0.0029.
Values may be sent and summed in bfloat16 or wider, within the bound.
No kernel may reach another device: no remote copies, remote signals or barrier semaphores. Data moves between devices by JAX's collectives and lax.ppermute only.
A program may use at most 64 MiB of HBM per device.

```python
import jax
import jax.numpy as jnp
from jax import lax

B = 192
NB_DEV = 8
NEIGH = 4
GMAX = 4
CAP = 56
RANKS = 1024
NCLUST = 256
NBLK = 1792
N_MESH = 32


def draw_block_counts(key, part):
    first_key = jax.random.fold_in(key, 11)
    second_key = jax.random.fold_in(key, 12)
    third_key = jax.random.fold_in(key, 13)
    drawn = jax.random.randint(first_key, (N_MESH,), CAP // 4, CAP + 1)
    fullest = jax.random.randint(second_key, (), 0, N_MESH)
    lightest = (fullest + 1 + jax.random.randint(third_key, (), 0, N_MESH - 1)) % N_MESH
    positions = jnp.arange(N_MESH)
    counts = jnp.where(positions == fullest, CAP, drawn)
    counts = jnp.where(positions == lightest, CAP // 4, counts)
    return counts.astype(jnp.int32)


def plant(values, key, least, top_value):
    spot = [jax.random.randint(jax.random.fold_in(key, axis), (), 0, length) for axis, length in enumerate(values.shape)]
    widest = values.shape.index(max(values.shape))
    beside = spot[:widest] + [(spot[widest] + 1) % values.shape[widest]] + spot[widest + 1:]
    return values.at[tuple(spot)].set(least).at[tuple(beside)].set(top_value)


def steps_of(stream_key, extent, cuts, smallest, high):
    def one(axis_at, blocks):
        heights = jax.random.uniform(jax.random.fold_in(jax.random.fold_in(stream_key, 6), axis_at), (blocks,), jnp.float32, smallest / len(cuts), high / len(cuts))
        return jnp.repeat(jnp.exp(heights), extent[axis_at] // blocks).reshape((-1,) + (1,) * (len(extent) - axis_at - 1))

    level = one(*cuts[0])
    for cut in cuts[1:]:
        level = level * one(*cut)
    return level


def normal_values(stream_key, dims, spread, limit, pieces=(), held_as=jnp.bfloat16):
    values = jax.random.normal(stream_key, dims, jnp.float32) * spread
    if len(pieces) > 0:
        values = steps_of(stream_key, dims, pieces, -0.22, 0.18) * values
    return jnp.clip(values, min=-limit, max=limit).astype(held_as)


def setup_inputs(seed: int = 0) -> dict:
    splits = jax.random.split(jax.random.key(seed), 8)
    return {
        "basis_vectors": normal_values(splits[0], (NCLUST, RANKS, B), (2.0 * (NCLUST * B) ** -0.25), 0.75, ((0, 32), (1, 16))),
        "stiffness_blocks": normal_values(splits[1], (NBLK, B, B), (4 * B) ** -0.5, 0.21875, ((0, 32),)),
        "block_rows": plant(jax.random.randint(splits[2], (NBLK,), 0, NB_DEV), jax.random.fold_in(splits[2], 1), 0, NB_DEV - 1).astype(jnp.int32),
        "block_columns": plant(jax.random.randint(splits[3], (NBLK,), 0, NB_DEV + NEIGH * GMAX), jax.random.fold_in(splits[3], 1), 0, (NB_DEV + NEIGH * GMAX) - 1).astype(jnp.int32),
        "density": jnp.clip(0.1 + 0.9 * jax.random.uniform(splits[4], (NBLK,), jnp.float32) ** steps_of(splits[4], (NBLK,), ((0, 32),), -0.2, 0.2), 0.1, 1.0),
        "block_counts": draw_block_counts(jax.random.fold_in(splits[7], 71), 0),
        "send_list": plant(jax.random.randint(splits[6], (N_MESH * NEIGH * GMAX,), 0, NB_DEV), jax.random.fold_in(splits[6], 1), 0, NB_DEV - 1).astype(jnp.int32),
    }


neighbour_offsets = (1, -1, 2, -2)


def reference(basis_vectors, stiffness_blocks, block_rows, block_columns, density, block_counts, send_list):
    offsets = jnp.array(neighbour_offsets, jnp.int32)
    sends = send_list.reshape(N_MESH, NEIGH, GMAX)

    def one_part(running, partition):
        first_block = (partition * CAP).astype(jnp.int32)
        part_blocks = lax.dynamic_slice_in_dim(stiffness_blocks, first_block, CAP, 0)
        rows_here = lax.dynamic_slice_in_dim(block_rows, first_block, CAP, 0)
        columns = lax.dynamic_slice_in_dim(block_columns, first_block, CAP, 0)
        density_here = lax.dynamic_slice_in_dim(density, first_block, CAP, 0)
        ghost_slot = jnp.maximum(columns - NB_DEV, 0)
        neighbour = ghost_slot // GMAX
        within = ghost_slot % GMAX
        sender = (partition - offsets[neighbour]) % N_MESH
        ghost_cluster = sender * NB_DEV + sends[sender, neighbour, within]
        source = jnp.where(columns < NB_DEV, partition * NB_DEV + columns, ghost_cluster).astype(jnp.int32)
        sources = basis_vectors[source].astype(jnp.float32)
        product = jnp.einsum("bpj,bij->bpi", sources, part_blocks.astype(jnp.float32), precision=lax.Precision.HIGHEST)
        active = jnp.arange(CAP, dtype=jnp.int32) < block_counts[partition]
        scale = jnp.where(active, 1e-3 + density_here ** 3, jnp.float32(0.0))
        selector = (rows_here[None, :] == jnp.arange(NB_DEV, dtype=jnp.int32)[:, None]).astype(jnp.float32) * scale[None, :]
        products = jnp.einsum("nb,bpi->npi", selector, product, precision=lax.Precision.HIGHEST).astype(jnp.bfloat16)
        own_slabs = lax.dynamic_slice_in_dim(basis_vectors, (partition * NB_DEV).astype(jnp.int32), NB_DEV, 0)
        tile = jnp.einsum("npc,nqc->pq", own_slabs.astype(jnp.float32), products.astype(jnp.float32), precision=lax.Precision.HIGHEST)
        return running + tile, None

    reduced, unused = lax.scan(one_part, jnp.zeros((RANKS, RANKS), jnp.float32), jnp.arange(N_MESH, dtype=jnp.int32))
    return reduced
```

```python
import functools

import jax
import jax.numpy as jnp
from jax import lax
from jax.experimental import pallas as pl
from jax.experimental.pallas import tpu as pltpu
from jax.sharding import Mesh
from jax.sharding import PartitionSpec as P

GMAX = 4
NEIGH = 4
DOFS = 192
OWN = 8
WIDTH = 64
CAP = 56
CHUNK = 8
PACKED = OWN * DOFS

neighbour_offsets = (1, -1, 2, -2)
VMEM = pl.BlockSpec(memory_space=pltpu.VMEM)
SMEM = pl.BlockSpec(memory_space=pltpu.SMEM)


def pack_pair(first, second, out_ref, at):
    dtype = out_ref.dtype
    out_ref[:, at : at + 128] = first[:, :128].astype(dtype)
    out_ref[:, at + 128 : at + 256] = second[:, :128].astype(dtype)
    rest = jnp.concatenate([first[:, 128:], second[:, 128:]], axis=1)
    out_ref[:, at + 256 : at + 384] = rest.astype(dtype)


def select_kernel(send_ref, basis_ref, packed_ref, *ghost_refs):
    for neighbour, ghost_ref in enumerate(ghost_refs):
        for pair in range(GMAX // 2):
            at = neighbour * GMAX + 2 * pair
            pack_pair(
                basis_ref[send_ref[at]], basis_ref[send_ref[at + 1]], ghost_ref, 384 * pair
            )
    for pair in range(OWN // 2):
        pack_pair(basis_ref[2 * pair], basis_ref[2 * pair + 1], packed_ref, 384 * pair)


def block_kernel(
    rows_ref, columns_ref, density_ref, count_ref, basis_ref, *rest
):
    ghost_refs = rest[:NEIGH]
    blocks_hbm, out_ref, blocks, pool, total, arrived = rest[NEIGH:]
    copies = []
    for chunk in range(CAP // CHUNK):
        part = pl.ds(chunk * CHUNK, CHUNK)
        copies.append(
            pltpu.make_async_copy(blocks_hbm.at[part], blocks.at[part], arrived.at[chunk])
        )
        copies[-1].start()
    pool[:OWN] = basis_ref[...]
    for neighbour, ghost_ref in enumerate(ghost_refs):
        for pair in range(GMAX // 2):
            at, slot = 384 * pair, OWN + neighbour * GMAX + 2 * pair
            pool[slot, :, :128] = ghost_ref[:, at : at + 128]
            pool[slot + 1, :, :128] = ghost_ref[:, at + 128 : at + 256]
            pool[slot, :, 128:] = ghost_ref[:, at + 256 : at + 320]
            pool[slot + 1, :, 128:] = ghost_ref[:, at + 320 : at + 384]
    total[...] = jnp.zeros_like(total)
    count = count_ref[0]
    for chunk in range(CAP // CHUNK):
        copies[chunk].wait()
        for block in range(chunk * CHUNK, (chunk + 1) * CHUNK):
            density = density_ref[block]
            scale = jnp.where(block < count, 0.001 + density * density * density, 0.0)
            product = lax.dot_general(
                pool[columns_ref[block]],
                blocks[block],
                (((1,), (1,)), ((), ())),
                preferred_element_type=jnp.float32,
            )
            row = rows_ref[block]
            total[row] = total[row] + scale * product
    for pair in range(OWN // 2):
        pack_pair(total[2 * pair], total[2 * pair + 1], out_ref, 384 * pair)


def tile_kernel(half_ref, rows_ref, own_ref, other_ref, out_ref):
    half = half_ref[0]
    low_lanes = lax.broadcasted_iota(jnp.int32, (16, 128), 1) < WIDTH
    for index, ref in ((half, own_ref), (1 - half, other_ref)):
        tile = lax.dot_general(
            ref[...], rows_ref[...], (((1,), (1,)), ((), ())), preferred_element_type=jnp.float32
        )
        for h in range(2):
            for x in range(4):
                low = tile[32 * h : 32 * h + 16, 128 * x : 128 * x + 128]
                high = tile[32 * h + 16 : 32 * h + 32, 128 * x : 128 * x + 128]
                low_turned = pltpu.roll(low, WIDTH, 1)
                high_turned = pltpu.roll(high, WIDTH, 1)
                at = 16 * index + 4 * x + h
                out_ref[at] = jnp.where(low_lanes, low, high_turned).astype(out_ref.dtype)
                out_ref[at + 2] = jnp.where(low_lanes, low_turned, high).astype(out_ref.dtype)


def sum_kernel(parts_ref, out_ref):
    total = jnp.sum(parts_ref[...].astype(jnp.float32), axis=0)
    out_ref[:16] = total[:, :WIDTH]
    out_ref[16:] = total[:, WIDTH:]


def local(
    basis_vectors, stiffness_blocks, block_rows, block_columns, density, block_counts, send_list
):
    mesh_axes, whole = ("y", "z_lo"), ("y", "z_lo", "z_hi", "x", "core")
    parts = lax.axis_size(mesh_axes)
    shape = jax.ShapeDtypeStruct
    packed, *picked = pl.pallas_call(
        select_kernel,
        out_shape=[shape((WIDTH, PACKED), jnp.bfloat16)]
        + [shape((WIDTH, GMAX * DOFS), jnp.bfloat16)] * NEIGH,
        in_specs=[SMEM, VMEM],
        out_specs=[VMEM] * (1 + NEIGH),
        name="select",
    )(send_list, basis_vectors)
    basis_rows = lax.all_gather(packed, ("x", "core"), axis=0, tiled=True)
    arriving = []
    for block, offset in zip(picked, neighbour_offsets):
        route = [((i - offset) % parts, i) for i in range(parts)]
        arriving.append(lax.ppermute(block, mesh_axes, route))
    products = pl.pallas_call(
        block_kernel,
        out_shape=shape((WIDTH, PACKED), jnp.bfloat16),
        in_specs=[SMEM] * 4 + [VMEM] * (1 + NEIGH) + [pl.BlockSpec(memory_space=pl.ANY)],
        out_specs=VMEM,
        scratch_shapes=[
            pltpu.VMEM((CAP, DOFS, DOFS), jnp.bfloat16),
            pltpu.VMEM((OWN + NEIGH * GMAX, WIDTH, DOFS), jnp.bfloat16),
            pltpu.VMEM((OWN, WIDTH, DOFS), jnp.float32),
            pltpu.SemaphoreType.DMA((CAP // CHUNK,)),
        ],
        compiler_params=pltpu.CompilerParams(vmem_limit_bytes=32 << 20),
        name="blocks",
    )(block_rows, block_columns, density, block_counts, basis_vectors, *arriving, stiffness_blocks)
    other = lax.ppermute(products, "z_hi", [(0, 1), (1, 0)])
    half = lax.axis_index("z_hi").astype(jnp.int32).reshape(1)
    chunks = pl.pallas_call(
        tile_kernel,
        out_shape=shape((parts, 16, 128), jnp.float32),
        in_specs=[SMEM] + [VMEM] * 3,
        out_specs=VMEM,
        compiler_params=pltpu.CompilerParams(vmem_limit_bytes=32 << 20),
        name="tile",
    )(half, basis_rows, products, other)
    shares = lax.all_to_all(chunks, mesh_axes, 0, 0, tiled=True)
    block = pl.pallas_call(
        sum_kernel,
        out_shape=shape((32, WIDTH), jnp.float32),
        in_specs=[VMEM],
        out_specs=VMEM,
        name="sum",
    )(shares)
    route = []
    for zh2 in range(2):
        for h in range(2):
            for zh in range(2):
                for a in range(8):
                    for b in range(8):
                        source = (zh2 * 16 + b * 2 + h) * 16 + zh * 8 + a
                        target = (zh2 * 16 + a * 2 + h) * 16 + zh * 8 + b
                        route.append((source, target))
    return lax.ppermute(block, whole, route).T


def solution(mesh):
    fine = Mesh(mesh.devices.reshape(8, 4, 2, 4, 2), ("y", "z_lo", "z_hi", "x", "core"))
    over_mesh, over_panel = ("y", "z_lo"), ("z_hi", "x", "core")
    placed = (
        P(over_mesh, over_panel, None),
        P(over_mesh, None, None),
        P(over_mesh),
        P(over_mesh),
        P(over_mesh),
        P(over_mesh),
        P(over_mesh),
    )
    return jax.shard_map(
        local, mesh=fine, in_specs=placed, out_specs=P(over_panel, over_mesh), check_vma=False
    )
```

```python
import functools

import jax
import jax.numpy as jnp
from jax import lax
from jax.experimental import pallas as pl
from jax.experimental.pallas import tpu as pltpu
from jax.sharding import Mesh
from jax.sharding import PartitionSpec as P

GMAX = 4
NEIGH = 4
DOFS = 192
OWN = 8
WIDTH = 64
CAP = 56
CHUNK = 8
PACKED = OWN * DOFS

neighbour_offsets = (1, -1, 2, -2)
x_offsets = (1, -1, 2)
VMEM = pl.BlockSpec(memory_space=pltpu.VMEM)
SMEM = pl.BlockSpec(memory_space=pltpu.SMEM)
HBM = pl.BlockSpec(memory_space=pltpu.HBM)


def pack_pair(first, second, out_ref, at):
    dtype = out_ref.dtype
    out_ref[:, at : at + 128] = first[:, :128].astype(dtype)
    out_ref[:, at + 128 : at + 256] = second[:, :128].astype(dtype)
    rest = jnp.concatenate([first[:, 128:], second[:, 128:]], axis=1)
    out_ref[:, at + 256 : at + 384] = rest.astype(dtype)


def select_kernel(send_ref, basis_ref, packed_ref, *ghost_refs):
    for neighbour, ghost_ref in enumerate(ghost_refs):
        for pair in range(GMAX // 2):
            at = neighbour * GMAX + 2 * pair
            pack_pair(
                basis_ref[send_ref[at]], basis_ref[send_ref[at + 1]], ghost_ref, 384 * pair
            )
    for pair in range(OWN // 2):
        pack_pair(basis_ref[2 * pair], basis_ref[2 * pair + 1], packed_ref, 384 * pair)


def block_kernel(
    rows_hbm, columns_hbm, density_hbm, count_hbm, basis_hbm, blocks_hbm, *rest
):
    ghost_refs = rest[:NEIGH]
    out_ref, rows_ref, columns_ref, density_ref, count_ref, blocks, pool, total, arrived, lists = rest[NEIGH:]
    small = [
        pltpu.make_async_copy(source, target, lists.at[index])
        for index, (source, target) in enumerate((
            (rows_hbm, rows_ref),
            (columns_hbm, columns_ref),
            (density_hbm, density_ref),
            (count_hbm, count_ref),
            (basis_hbm, pool.at[pl.ds(0, OWN)]),
        ))
    ]
    for copy in small:
        copy.start()
    copies = []
    for chunk in range(CAP // CHUNK):
        part = pl.ds(chunk * CHUNK, CHUNK)
        copies.append(
            pltpu.make_async_copy(blocks_hbm.at[part], blocks.at[part], arrived.at[chunk])
        )
        copies[-1].start()
    for neighbour, ghost_ref in enumerate(ghost_refs):
        for pair in range(GMAX // 2):
            at, slot = 384 * pair, OWN + neighbour * GMAX + 2 * pair
            pool[slot, :, :128] = ghost_ref[:, at : at + 128]
            pool[slot + 1, :, :128] = ghost_ref[:, at + 128 : at + 256]
            pool[slot, :, 128:] = ghost_ref[:, at + 256 : at + 320]
            pool[slot + 1, :, 128:] = ghost_ref[:, at + 320 : at + 384]
    total[...] = jnp.zeros_like(total)
    for copy in small:
        copy.wait()
    count = count_ref[0]
    for chunk in range(CAP // CHUNK):
        copies[chunk].wait()
        for block in range(chunk * CHUNK, (chunk + 1) * CHUNK):
            density = density_ref[block]
            scale = jnp.where(block < count, 0.001 + density * density * density, 0.0)
            product = lax.dot_general(
                pool[columns_ref[block]],
                blocks[block],
                (((1,), (1,)), ((), ())),
                preferred_element_type=jnp.float32,
            )
            row = rows_ref[block]
            total[row] = total[row] + scale * product
    for pair in range(OWN // 2):
        pack_pair(total[2 * pair], total[2 * pair + 1], out_ref, 384 * pair)


def tile_kernel(place_ref, *rest):
    *row_refs, own_ref, other_ref, out_ref = rest
    half, x, core = place_ref[0], place_ref[1], place_ref[2]
    low_lanes = lax.broadcasted_iota(jnp.int32, (16, 2 * WIDTH), 1) < WIDTH
    for index, ref in ((half, own_ref), (1 - half, other_ref)):
        for slot, offset in enumerate((0,) + x_offsets):
            rows = jnp.concatenate([row_refs[0][slot], row_refs[1][slot]], axis=0)
            tile = lax.dot_general(
                ref[...], rows, (((1,), (1,)), ((), ())), preferred_element_type=jnp.float32
            )
            for h in range(2):
                low, high = tile[32 * h : 32 * h + 16], tile[32 * h + 16 : 32 * h + 32]
                low_turned = pltpu.roll(low, WIDTH, 1)
                high_turned = pltpu.roll(high, WIDTH, 1)
                at = 16 * index + 4 * ((x - offset + 4) % 4) + h
                out_ref[at + 2 * core] = jnp.where(low_lanes, low, high_turned)
                out_ref[at + 2 - 2 * core] = jnp.where(low_lanes, low_turned, high)


def sum_kernel(parts_ref, out_ref):
    total = jnp.sum(parts_ref[...].astype(jnp.float32), axis=0)
    out_ref[:16] = total[:, :WIDTH]
    out_ref[16:] = total[:, WIDTH:]


def local(
    basis_vectors, stiffness_blocks, block_rows, block_columns, density, block_counts, send_list
):
    mesh_axes, whole = ("y", "z_lo"), ("y", "z_lo", "z_hi", "x", "core")
    parts = lax.axis_size(mesh_axes)
    shape = jax.ShapeDtypeStruct
    packed, *picked = pl.pallas_call(
        select_kernel,
        out_shape=[shape((WIDTH, PACKED), jnp.bfloat16)]
        + [shape((WIDTH, GMAX * DOFS), jnp.bfloat16)] * NEIGH,
        in_specs=[SMEM, VMEM],
        out_specs=[VMEM] * (1 + NEIGH),
        name="select",
    )(send_list, basis_vectors)
    arriving, gathered = [], [packed]
    for block, offset in zip(picked, neighbour_offsets):
        route = [((i - offset) % parts, i) for i in range(parts)]
        arriving.append(lax.ppermute(block, mesh_axes, route))
        if len(gathered) <= len(x_offsets):
            x_offset = x_offsets[len(gathered) - 1]
            route = [((i - x_offset) % 4, i) for i in range(4)]
            gathered.append(lax.ppermute(packed, "x", route))
    core_rows = jnp.stack(gathered)
    other_rows = lax.ppermute(core_rows, "core", [(0, 1), (1, 0)])
    products = pl.pallas_call(
        block_kernel,
        out_shape=shape((WIDTH, PACKED), jnp.bfloat16),
        in_specs=[HBM] * 6 + [VMEM] * NEIGH,
        out_specs=VMEM,
        scratch_shapes=[
            pltpu.SMEM((CAP,), jnp.int32),
            pltpu.SMEM((CAP,), jnp.int32),
            pltpu.SMEM((CAP,), jnp.float32),
            pltpu.SMEM((1,), jnp.int32),
            pltpu.VMEM((CAP, DOFS, DOFS), jnp.bfloat16),
            pltpu.VMEM((OWN + NEIGH * GMAX, WIDTH, DOFS), jnp.bfloat16),
            pltpu.VMEM((OWN, WIDTH, DOFS), jnp.float32),
            pltpu.SemaphoreType.DMA((CAP // CHUNK,)),
            pltpu.SemaphoreType.DMA((5,)),
        ],
        compiler_params=pltpu.CompilerParams(vmem_limit_bytes=64 << 20),
        name="blocks",
    )(block_rows, block_columns, density, block_counts, basis_vectors, stiffness_blocks, *arriving)
    other = lax.ppermute(products, "z_hi", [(0, 1), (1, 0)])
    place = jnp.stack([lax.axis_index(name) for name in ("z_hi", "x", "core")]).astype(jnp.int32)
    chunks = pl.pallas_call(
        tile_kernel,
        out_shape=shape((parts, 16, 128), jnp.float32),
        in_specs=[SMEM] + [VMEM] * 4,
        out_specs=VMEM,
        compiler_params=pltpu.CompilerParams(vmem_limit_bytes=64 << 20),
        name="tile",
    )(place, core_rows, other_rows, products, other)
    shares = lax.all_to_all(chunks, mesh_axes, 0, 0, tiled=True)
    block = pl.pallas_call(
        sum_kernel,
        out_shape=shape((32, WIDTH), jnp.float32),
        in_specs=[VMEM],
        out_specs=VMEM,
        name="sum",
    )(shares)
    route = []
    for zh2 in range(2):
        for h in range(2):
            for zh in range(2):
                for a in range(8):
                    for b in range(8):
                        source = (zh2 * 16 + b * 2 + h) * 16 + zh * 8 + a
                        target = (zh2 * 16 + a * 2 + h) * 16 + zh * 8 + b
                        route.append((source, target))
    return lax.ppermute(block, whole, route).T


def solution(mesh):
    fine = Mesh(mesh.devices.reshape(8, 4, 2, 4, 2), ("y", "z_lo", "z_hi", "x", "core"))
    over_mesh, over_panel = ("y", "z_lo"), ("z_hi", "x", "core")
    placed = (
        P(over_mesh, over_panel, None),
        P(over_mesh, None, None),
        P(over_mesh),
        P(over_mesh),
        P(over_mesh),
        P(over_mesh),
        P(over_mesh),
    )
    return jax.shard_map(
        local, mesh=fine, in_specs=placed, out_specs=P(over_panel, over_mesh), check_vma=False
    )
```

```python
import functools

import jax
import jax.numpy as jnp
from jax import lax
from jax.experimental import pallas as pl
from jax.experimental.pallas import tpu as pltpu
from jax.sharding import Mesh
from jax.sharding import PartitionSpec as P

GMAX = 4
NEIGH = 4
DOFS = 192
OWN = 8
WIDTH = 64
CAP = 56
CHUNK = 8
PACKED = OWN * DOFS

neighbour_offsets = (1, -1, 2, -2)
x_offsets = (1, -1, 2)
VMEM = pl.BlockSpec(memory_space=pltpu.VMEM)
SMEM = pl.BlockSpec(memory_space=pltpu.SMEM)
HBM = pl.BlockSpec(memory_space=pltpu.HBM)


def pack_pair(first, second, out_ref, at):
    dtype = out_ref.dtype
    out_ref[:, at : at + 128] = first[:, :128].astype(dtype)
    out_ref[:, at + 128 : at + 256] = second[:, :128].astype(dtype)
    rest = jnp.concatenate([first[:, 128:], second[:, 128:]], axis=1)
    out_ref[:, at + 256 : at + 384] = rest.astype(dtype)


def select_kernel(send_ref, basis_ref, packed_ref, *ghost_refs):
    for neighbour, ghost_ref in enumerate(ghost_refs):
        for pair in range(GMAX // 2):
            at = neighbour * GMAX + 2 * pair
            pack_pair(
                basis_ref[send_ref[at]], basis_ref[send_ref[at + 1]], ghost_ref, 384 * pair
            )
    for pair in range(OWN // 2):
        pack_pair(basis_ref[2 * pair], basis_ref[2 * pair + 1], packed_ref, 384 * pair)


def block_kernel(
    rows_hbm, columns_hbm, density_hbm, count_hbm, basis_hbm, blocks_hbm, *rest
):
    ghost_refs = rest[:NEIGH]
    out_ref, rows_ref, columns_ref, density_ref, count_ref, blocks, pool, total, arrived, lists = rest[NEIGH:]
    small = [
        pltpu.make_async_copy(source, target, lists.at[index])
        for index, (source, target) in enumerate((
            (rows_hbm, rows_ref),
            (columns_hbm, columns_ref),
            (density_hbm, density_ref),
            (count_hbm, count_ref),
            (basis_hbm, pool.at[pl.ds(0, OWN)]),
        ))
    ]
    for copy in small:
        copy.start()
    copies = []
    for chunk in range(CAP // CHUNK):
        part = pl.ds(chunk * CHUNK, CHUNK)
        copies.append(
            pltpu.make_async_copy(blocks_hbm.at[part], blocks.at[part], arrived.at[chunk])
        )
        copies[-1].start()
    for neighbour, ghost_ref in enumerate(ghost_refs):
        for pair in range(GMAX // 2):
            at, slot = 384 * pair, OWN + neighbour * GMAX + 2 * pair
            pool[slot, :, :128] = ghost_ref[:, at : at + 128]
            pool[slot + 1, :, :128] = ghost_ref[:, at + 128 : at + 256]
            pool[slot, :, 128:] = ghost_ref[:, at + 256 : at + 320]
            pool[slot + 1, :, 128:] = ghost_ref[:, at + 320 : at + 384]
    total[...] = jnp.zeros_like(total)
    for copy in small:
        copy.wait()
    count = count_ref[0]
    for chunk in range(CAP // CHUNK):
        copies[chunk].wait()
        for block in range(chunk * CHUNK, (chunk + 1) * CHUNK):
            density = density_ref[block]
            scale = jnp.where(block < count, 0.001 + density * density * density, 0.0)
            product = lax.dot_general(
                pool[columns_ref[block]],
                blocks[block],
                (((1,), (1,)), ((), ())),
                preferred_element_type=jnp.float32,
            )
            row = rows_ref[block]
            total[row] = total[row] + scale * product
    for pair in range(OWN // 2):
        pack_pair(total[2 * pair], total[2 * pair + 1], out_ref, 384 * pair)


def tile_kernel(place_ref, *rest):
    *row_refs, own_ref, other_ref, out_ref = rest
    half, x, core = place_ref[0], place_ref[1], place_ref[2]
    low_lanes = lax.broadcasted_iota(jnp.int32, (16, 2 * WIDTH), 1) < WIDTH
    for index, ref in ((half, own_ref), (1 - half, other_ref)):
        for slot, offset in enumerate((0,) + x_offsets):
            tile = lax.dot_general(
                ref[...],
                row_refs[slot][...],
                (((1,), (1,)), ((), ())),
                preferred_element_type=jnp.float32,
            )
            for h in range(2):
                low, high = tile[32 * h : 32 * h + 16], tile[32 * h + 16 : 32 * h + 32]
                low_turned = pltpu.roll(low, WIDTH, 1)
                high_turned = pltpu.roll(high, WIDTH, 1)
                at = 16 * index + 4 * ((x - offset + 4) % 4) + h
                out_ref[at + 2 * core] = jnp.where(low_lanes, low, high_turned)
                out_ref[at + 2 - 2 * core] = jnp.where(low_lanes, low_turned, high)


def sum_kernel(parts_ref, out_ref):
    total = jnp.sum(parts_ref[...].astype(jnp.float32), axis=0)
    out_ref[:16] = total[:, :WIDTH]
    out_ref[16:] = total[:, WIDTH:]


def local(
    basis_vectors, stiffness_blocks, block_rows, block_columns, density, block_counts, send_list
):
    mesh_axes, whole = ("y", "z_lo"), ("y", "z_lo", "z_hi", "x", "core")
    parts = lax.axis_size(mesh_axes)
    shape = jax.ShapeDtypeStruct
    packed, *picked = pl.pallas_call(
        select_kernel,
        out_shape=[shape((WIDTH, PACKED), jnp.bfloat16)]
        + [shape((WIDTH, GMAX * DOFS), jnp.bfloat16)] * NEIGH,
        in_specs=[SMEM, VMEM],
        out_specs=[VMEM] * (1 + NEIGH),
        name="select",
    )(send_list, basis_vectors)
    other_packed = lax.ppermute(packed, "core", [(0, 1), (1, 0)])
    arriving = []
    for block, offset in zip(picked, neighbour_offsets):
        route = [((i - offset) % parts, i) for i in range(parts)]
        arriving.append(lax.ppermute(block, mesh_axes, route))
    pair = jnp.concatenate([packed, other_packed])
    basis_rows = [pair]
    for offset in x_offsets:
        basis_rows.append(lax.ppermute(pair, "x", [((i - offset) % 4, i) for i in range(4)]))
    products = pl.pallas_call(
        block_kernel,
        out_shape=shape((WIDTH, PACKED), jnp.bfloat16),
        in_specs=[HBM] * 6 + [VMEM] * NEIGH,
        out_specs=VMEM,
        scratch_shapes=[
            pltpu.SMEM((CAP,), jnp.int32),
            pltpu.SMEM((CAP,), jnp.int32),
            pltpu.SMEM((CAP,), jnp.float32),
            pltpu.SMEM((1,), jnp.int32),
            pltpu.VMEM((CAP, DOFS, DOFS), jnp.bfloat16),
            pltpu.VMEM((OWN + NEIGH * GMAX, WIDTH, DOFS), jnp.bfloat16),
            pltpu.VMEM((OWN, WIDTH, DOFS), jnp.float32),
            pltpu.SemaphoreType.DMA((CAP // CHUNK,)),
            pltpu.SemaphoreType.DMA((5,)),
        ],
        compiler_params=pltpu.CompilerParams(vmem_limit_bytes=64 << 20),
        name="blocks",
    )(block_rows, block_columns, density, block_counts, basis_vectors, stiffness_blocks, *arriving)
    other = lax.ppermute(products, "z_hi", [(0, 1), (1, 0)])
    place = jnp.stack([lax.axis_index(name) for name in ("z_hi", "x", "core")]).astype(jnp.int32)
    chunks = pl.pallas_call(
        tile_kernel,
        out_shape=shape((parts, 16, 128), jnp.float32),
        in_specs=[SMEM] + [VMEM] * 6,
        out_specs=VMEM,
        compiler_params=pltpu.CompilerParams(vmem_limit_bytes=64 << 20),
        name="tile",
    )(place, *basis_rows, products, other)
    shares = lax.all_to_all(chunks, mesh_axes, 0, 0, tiled=True)
    block = pl.pallas_call(
        sum_kernel,
        out_shape=shape((32, WIDTH), jnp.float32),
        in_specs=[VMEM],
        out_specs=VMEM,
        name="sum",
    )(shares)
    route = []
    for zh2 in range(2):
        for h in range(2):
            for zh in range(2):
                for a in range(8):
                    for b in range(8):
                        source = (zh2 * 16 + b * 2 + h) * 16 + zh * 8 + a
                        target = (zh2 * 16 + a * 2 + h) * 16 + zh * 8 + b
                        route.append((source, target))
    return lax.ppermute(block, whole, route).T


def solution(mesh):
    fine = Mesh(mesh.devices.reshape(8, 4, 2, 4, 2), ("y", "z_lo", "z_hi", "x", "core"))
    over_mesh, over_panel = ("y", "z_lo"), ("z_hi", "x", "core")
    placed = (
        P(over_mesh, over_panel, None),
        P(over_mesh, None, None),
        P(over_mesh),
        P(over_mesh),
        P(over_mesh),
        P(over_mesh),
        P(over_mesh),
    )
    return jax.shard_map(
        local, mesh=fine, in_specs=placed, out_specs=P(over_panel, over_mesh), check_vma=False
    )
```

```python
import functools

import jax
import jax.numpy as jnp
from jax import lax
from jax.experimental import pallas as pl
from jax.experimental.pallas import tpu as pltpu
from jax.sharding import Mesh
from jax.sharding import PartitionSpec as P

GMAX = 4
NEIGH = 4
DOFS = 192
OWN = 8
WIDTH = 64
CAP = 56
CHUNK = 8
PACKED = OWN * DOFS

neighbour_offsets = (1, -1, 2, -2)
x_offsets = (1, -1, 2)
VMEM = pl.BlockSpec(memory_space=pltpu.VMEM)
SMEM = pl.BlockSpec(memory_space=pltpu.SMEM)
HBM = pl.BlockSpec(memory_space=pltpu.HBM)


def pack_pair(first, second, out_ref, at):
    dtype = out_ref.dtype
    out_ref[:, at : at + 128] = first[:, :128].astype(dtype)
    out_ref[:, at + 128 : at + 256] = second[:, :128].astype(dtype)
    rest = jnp.concatenate([first[:, 128:], second[:, 128:]], axis=1)
    out_ref[:, at + 256 : at + 384] = rest.astype(dtype)


def select_kernel(send_ref, basis_ref, packed_ref, *ghost_refs):
    for neighbour, ghost_ref in enumerate(ghost_refs):
        for pair in range(GMAX // 2):
            at = neighbour * GMAX + 2 * pair
            pack_pair(
                basis_ref[send_ref[at]], basis_ref[send_ref[at + 1]], ghost_ref, 384 * pair
            )
    for pair in range(OWN // 2):
        pack_pair(basis_ref[2 * pair], basis_ref[2 * pair + 1], packed_ref, 384 * pair)


def block_kernel(
    rows_hbm, columns_hbm, density_hbm, count_hbm, basis_hbm, blocks_hbm, *rest
):
    ghost_refs = rest[:NEIGH]
    out_ref, rows_ref, columns_ref, density_ref, count_ref, blocks, pool, total, arrived, lists = rest[NEIGH:]
    small = [
        pltpu.make_async_copy(source, target, lists.at[index])
        for index, (source, target) in enumerate((
            (rows_hbm, rows_ref),
            (columns_hbm, columns_ref),
            (density_hbm, density_ref),
            (count_hbm, count_ref),
            (basis_hbm, pool.at[pl.ds(0, OWN)]),
        ))
    ]
    for copy in small:
        copy.start()
    copies = []
    for chunk in range(CAP // CHUNK):
        part = pl.ds(chunk * CHUNK, CHUNK)
        copies.append(
            pltpu.make_async_copy(blocks_hbm.at[part], blocks.at[part], arrived.at[chunk])
        )
        copies[-1].start()
    for neighbour, ghost_ref in enumerate(ghost_refs):
        for pair in range(GMAX // 2):
            at, slot = 384 * pair, OWN + neighbour * GMAX + 2 * pair
            pool[slot, :, :128] = ghost_ref[:, at : at + 128]
            pool[slot + 1, :, :128] = ghost_ref[:, at + 128 : at + 256]
            pool[slot, :, 128:] = ghost_ref[:, at + 256 : at + 320]
            pool[slot + 1, :, 128:] = ghost_ref[:, at + 320 : at + 384]
    total[...] = jnp.zeros_like(total)
    for copy in small:
        copy.wait()
    count = count_ref[0]
    for chunk in range(CAP // CHUNK):
        copies[chunk].wait()
        for block in range(chunk * CHUNK, (chunk + 1) * CHUNK):
            density = density_ref[block]
            scale = jnp.where(block < count, 0.001 + density * density * density, 0.0)
            product = lax.dot_general(
                pool[columns_ref[block]],
                blocks[block],
                (((1,), (1,)), ((), ())),
                preferred_element_type=jnp.float32,
            )
            row = rows_ref[block]
            total[row] = total[row] + scale * product
    for pair in range(OWN // 2):
        pack_pair(total[2 * pair], total[2 * pair + 1], out_ref, 384 * pair)


def tile_kernel(place_ref, *rest):
    *row_refs, own_ref, other_ref, out_ref = rest
    half, x, core = place_ref[0], place_ref[1], place_ref[2]
    low_lanes = lax.broadcasted_iota(jnp.int32, (16, 2 * WIDTH), 1) < WIDTH
    for column, ref in ((core, own_ref), (1 - core, other_ref)):
        for slot, offset in enumerate((0,) + x_offsets):
            tile = lax.dot_general(
                ref[...],
                row_refs[slot][...],
                (((1,), (1,)), ((), ())),
                preferred_element_type=jnp.float32,
            )
            for h in range(2):
                low, high = tile[32 * h : 32 * h + 16], tile[32 * h + 16 : 32 * h + 32]
                low_turned = pltpu.roll(low, WIDTH, 1)
                high_turned = pltpu.roll(high, WIDTH, 1)
                at = 4 * ((x - offset + 4) % 4) + 2 * column + h
                out_ref[16 * half + at] = jnp.where(low_lanes, low, high_turned)
                out_ref[16 - 16 * half + at] = jnp.where(low_lanes, low_turned, high)


def sum_kernel(parts_ref, out_ref):
    total = jnp.sum(parts_ref[...].astype(jnp.float32), axis=0)
    out_ref[:16] = total[:, :WIDTH]
    out_ref[16:] = total[:, WIDTH:]


def local(
    basis_vectors, stiffness_blocks, block_rows, block_columns, density, block_counts, send_list
):
    mesh_axes, whole = ("y", "z_lo"), ("y", "z_lo", "z_hi", "x", "core")
    parts = lax.axis_size(mesh_axes)
    shape = jax.ShapeDtypeStruct
    packed, *picked = pl.pallas_call(
        select_kernel,
        out_shape=[shape((WIDTH, PACKED), jnp.bfloat16)]
        + [shape((WIDTH, GMAX * DOFS), jnp.bfloat16)] * NEIGH,
        in_specs=[SMEM, VMEM],
        out_specs=[VMEM] * (1 + NEIGH),
        name="select",
    )(send_list, basis_vectors)
    other_packed = lax.ppermute(packed, "z_hi", [(0, 1), (1, 0)])
    arriving = []
    for block, offset in zip(picked, neighbour_offsets):
        route = [((i - offset) % parts, i) for i in range(parts)]
        arriving.append(lax.ppermute(block, mesh_axes, route))
    pair = jnp.concatenate([packed, other_packed])
    pair, _ = lax.optimization_barrier((pair, arriving[0]))
    basis_rows = [pair]
    for offset in x_offsets:
        basis_rows.append(lax.ppermute(pair, "x", [((i - offset) % 4, i) for i in range(4)]))
    products = pl.pallas_call(
        block_kernel,
        out_shape=shape((WIDTH, PACKED), jnp.bfloat16),
        in_specs=[HBM] * 6 + [VMEM] * NEIGH,
        out_specs=VMEM,
        scratch_shapes=[
            pltpu.SMEM((CAP,), jnp.int32),
            pltpu.SMEM((CAP,), jnp.int32),
            pltpu.SMEM((CAP,), jnp.float32),
            pltpu.SMEM((1,), jnp.int32),
            pltpu.VMEM((CAP, DOFS, DOFS), jnp.bfloat16),
            pltpu.VMEM((OWN + NEIGH * GMAX, WIDTH, DOFS), jnp.bfloat16),
            pltpu.VMEM((OWN, WIDTH, DOFS), jnp.float32),
            pltpu.SemaphoreType.DMA((CAP // CHUNK,)),
            pltpu.SemaphoreType.DMA((5,)),
        ],
        compiler_params=pltpu.CompilerParams(vmem_limit_bytes=64 << 20),
        name="blocks",
    )(block_rows, block_columns, density, block_counts, basis_vectors, stiffness_blocks, *arriving)
    other = lax.ppermute(products, "core", [(0, 1), (1, 0)])
    place = jnp.stack([lax.axis_index(name) for name in ("z_hi", "x", "core")]).astype(jnp.int32)
    chunks = pl.pallas_call(
        tile_kernel,
        out_shape=shape((parts, 16, 128), jnp.float32),
        in_specs=[SMEM] + [VMEM] * 6,
        out_specs=VMEM,
        compiler_params=pltpu.CompilerParams(vmem_limit_bytes=64 << 20),
        name="tile",
    )(place, *basis_rows, products, other)
    shares = lax.all_to_all(chunks, mesh_axes, 0, 0, tiled=True)
    block = pl.pallas_call(
        sum_kernel,
        out_shape=shape((32, WIDTH), jnp.float32),
        in_specs=[VMEM],
        out_specs=VMEM,
        name="sum",
    )(shares)
    route = []
    for a in range(8):
        for b in range(8):
            for rest in range(4):
                for core in range(2):
                    source = (a * 4 + rest) * 16 + b * 2 + core
                    target = (b * 4 + rest) * 16 + a * 2 + core
                    route.append((source, target))
    return lax.ppermute(block, whole, route).T


def solution(mesh):
    fine = Mesh(mesh.devices.reshape(8, 4, 2, 4, 2), ("y", "z_lo", "z_hi", "x", "core"))
    over_mesh, over_panel = ("y", "z_lo"), ("z_hi", "x", "core")
    placed = (
        P(over_mesh, over_panel, None),
        P(over_mesh, None, None),
        P(over_mesh),
        P(over_mesh),
        P(over_mesh),
        P(over_mesh),
        P(over_mesh),
    )
    return jax.shard_map(
        local, mesh=fine, in_specs=placed, out_specs=P(over_panel, over_mesh), check_vma=False
    )
```

```python
import functools

import jax
import jax.numpy as jnp
from jax import lax
from jax.experimental import pallas as pl
from jax.experimental.pallas import tpu as pltpu
from jax.sharding import Mesh
from jax.sharding import PartitionSpec as P

GMAX = 4
NEIGH = 4
DOFS = 192
OWN = 8
WIDTH = 64
CAP = 56
CHUNK = 8
PACKED = OWN * DOFS

neighbour_offsets = (1, -1, 2, -2)
x_offsets = (1, -1, 2)
VMEM = pl.BlockSpec(memory_space=pltpu.VMEM)
SMEM = pl.BlockSpec(memory_space=pltpu.SMEM)
HBM = pl.BlockSpec(memory_space=pltpu.HBM)


def pack_pair(first, second, out_ref, at):
    dtype = out_ref.dtype
    out_ref[:, at : at + 128] = first[:, :128].astype(dtype)
    out_ref[:, at + 128 : at + 256] = second[:, :128].astype(dtype)
    rest = jnp.concatenate([first[:, 128:], second[:, 128:]], axis=1)
    out_ref[:, at + 256 : at + 384] = rest.astype(dtype)


def select_kernel(send_ref, basis_ref, packed_ref, *ghost_refs):
    for neighbour, ghost_ref in enumerate(ghost_refs):
        for pair in range(GMAX // 2):
            at = neighbour * GMAX + 2 * pair
            pack_pair(
                basis_ref[send_ref[at]], basis_ref[send_ref[at + 1]], ghost_ref, 384 * pair
            )
    for pair in range(OWN // 2):
        pack_pair(basis_ref[2 * pair], basis_ref[2 * pair + 1], packed_ref, 384 * pair)


def block_kernel(
    rows_hbm, columns_hbm, density_hbm, count_hbm, basis_hbm, blocks_hbm, *rest
):
    ghost_refs = rest[:NEIGH]
    out_ref, rows_ref, columns_ref, density_ref, count_ref, blocks, pool, total, arrived, lists = rest[NEIGH:]
    small = [
        pltpu.make_async_copy(source, target, lists.at[index])
        for index, (source, target) in enumerate((
            (rows_hbm, rows_ref),
            (columns_hbm, columns_ref),
            (density_hbm, density_ref),
            (count_hbm, count_ref),
            (basis_hbm, pool.at[pl.ds(0, OWN)]),
        ))
    ]
    for copy in small:
        copy.start()
    copies = []
    for chunk in range(CAP // CHUNK):
        part = pl.ds(chunk * CHUNK, CHUNK)
        copies.append(
            pltpu.make_async_copy(blocks_hbm.at[part], blocks.at[part], arrived.at[chunk])
        )
        copies[-1].start()
    for neighbour, ghost_ref in enumerate(ghost_refs):
        for pair in range(GMAX // 2):
            at, slot = 384 * pair, OWN + neighbour * GMAX + 2 * pair
            pool[slot, :, :128] = ghost_ref[:, at : at + 128]
            pool[slot + 1, :, :128] = ghost_ref[:, at + 128 : at + 256]
            pool[slot, :, 128:] = ghost_ref[:, at + 256 : at + 320]
            pool[slot + 1, :, 128:] = ghost_ref[:, at + 320 : at + 384]
    total[...] = jnp.zeros_like(total)
    for copy in small:
        copy.wait()
    count = count_ref[0]
    for chunk in range(CAP // CHUNK):
        copies[chunk].wait()
        for block in range(chunk * CHUNK, (chunk + 1) * CHUNK):
            density = density_ref[block]
            scale = jnp.where(block < count, 0.001 + density * density * density, 0.0)
            product = lax.dot_general(
                pool[columns_ref[block]],
                blocks[block],
                (((1,), (1,)), ((), ())),
                preferred_element_type=jnp.float32,
            )
            row = rows_ref[block]
            total[row] = total[row] + scale * product
    for pair in range(OWN // 2):
        pack_pair(total[2 * pair], total[2 * pair + 1], out_ref, 384 * pair)


def tile_kernel(place_ref, *rest):
    row_refs, product_refs, out_ref = rest[:4], rest[4:8], rest[8]
    half, x, core = place_ref[0], place_ref[1], place_ref[2]
    low_lanes = lax.broadcasted_iota(jnp.int32, (16, 2 * WIDTH), 1) < WIDTH
    row_places = [(x - offset + 4) % 4 for offset in (0,) + x_offsets]
    column_places = [(half, core), (1 - half, core), (half, 1 - core), (1 - half, 1 - core)]
    for slot in (0, 2):
        rows = jnp.concatenate([row_refs[slot][...], row_refs[slot + 1][...]], axis=0)
        for (z_place, core_place), ref in zip(column_places, product_refs):
            tile = lax.dot_general(
                ref[...], rows, (((1,), (1,)), ((), ())), preferred_element_type=jnp.float32
            )
            for h in range(2):
                low, high = tile[32 * h : 32 * h + 16], tile[32 * h + 16 : 32 * h + 32]
                low_turned = pltpu.roll(low, WIDTH, 1)
                high_turned = pltpu.roll(high, WIDTH, 1)
                at = 16 * z_place + 2 * core_place + h
                out_ref[at + 4 * row_places[slot]] = jnp.where(low_lanes, low, high_turned)
                out_ref[at + 4 * row_places[slot + 1]] = jnp.where(low_lanes, low_turned, high)


def sum_kernel(parts_ref, out_ref):
    total = jnp.sum(parts_ref[...].astype(jnp.float32), axis=0)
    out_ref[:16] = total[:, :WIDTH]
    out_ref[16:] = total[:, WIDTH:]


def local(
    basis_vectors, stiffness_blocks, block_rows, block_columns, density, block_counts, send_list
):
    mesh_axes, whole = ("y", "z_lo"), ("y", "z_lo", "z_hi", "x", "core")
    parts = lax.axis_size(mesh_axes)
    shape = jax.ShapeDtypeStruct
    packed, *picked = pl.pallas_call(
        select_kernel,
        out_shape=[shape((WIDTH, PACKED), jnp.bfloat16)]
        + [shape((WIDTH, GMAX * DOFS), jnp.bfloat16)] * NEIGH,
        in_specs=[SMEM, VMEM],
        out_specs=[VMEM] * (1 + NEIGH),
        name="select",
    )(send_list, basis_vectors)
    arriving = []
    for block, offset in zip(picked, neighbour_offsets):
        route = [((i - offset) % parts, i) for i in range(parts)]
        arriving.append(lax.ppermute(block, mesh_axes, route))
    products = pl.pallas_call(
        block_kernel,
        out_shape=shape((WIDTH, PACKED), jnp.bfloat16),
        in_specs=[HBM] * 6 + [VMEM] * NEIGH,
        out_specs=VMEM,
        scratch_shapes=[
            pltpu.SMEM((CAP,), jnp.int32),
            pltpu.SMEM((CAP,), jnp.int32),
            pltpu.SMEM((CAP,), jnp.float32),
            pltpu.SMEM((1,), jnp.int32),
            pltpu.VMEM((CAP, DOFS, DOFS), jnp.bfloat16),
            pltpu.VMEM((OWN + NEIGH * GMAX, WIDTH, DOFS), jnp.bfloat16),
            pltpu.VMEM((OWN, WIDTH, DOFS), jnp.float32),
            pltpu.SemaphoreType.DMA((CAP // CHUNK,)),
            pltpu.SemaphoreType.DMA((5,)),
        ],
        compiler_params=pltpu.CompilerParams(vmem_limit_bytes=64 << 20),
        name="blocks",
    )(block_rows, block_columns, density, block_counts, basis_vectors, stiffness_blocks, *arriving)
    swap = [(0, 1), (1, 0)]
    over_z = lax.ppermute(products, "z_hi", swap)
    over_core = lax.ppermute(products, "core", swap)
    over_both = lax.ppermute(over_z, "core", swap)
    packed, _ = lax.optimization_barrier((packed, products))
    basis_rows = [packed]
    for offset in x_offsets:
        basis_rows.append(lax.ppermute(packed, "x", [((i - offset) % 4, i) for i in range(4)]))
    place = jnp.stack([lax.axis_index(name) for name in ("z_hi", "x", "core")]).astype(jnp.int32)
    chunks = pl.pallas_call(
        tile_kernel,
        out_shape=shape((parts, 16, 128), jnp.float32),
        in_specs=[SMEM] + [VMEM] * 8,
        out_specs=VMEM,
        compiler_params=pltpu.CompilerParams(vmem_limit_bytes=8 << 20),
        name="tile",
    )(place, *basis_rows, products, over_z, over_core, over_both)
    shares = lax.all_to_all(chunks, mesh_axes, 0, 0, tiled=True)
    block = pl.pallas_call(
        sum_kernel,
        out_shape=shape((32, WIDTH), jnp.float32),
        in_specs=[VMEM],
        out_specs=VMEM,
        name="sum",
    )(shares)
    route = []
    for a in range(4):
        for b in range(4):
            for place2 in range(8):
                for panel in range(4):
                    z2, rest, z, c = place2 // 4, place2 % 4, panel // 2, panel % 2
                    source = (z2 * 16 + a * 4 + rest) * 16 + z * 8 + b * 2 + c
                    target = (z2 * 16 + b * 4 + rest) * 16 + z * 8 + a * 2 + c
                    route.append((source, target))

    return lax.ppermute(block, whole, route).T


def solution(mesh):
    fine = Mesh(mesh.devices.reshape(8, 4, 2, 4, 2), ("y", "z_lo", "z_hi", "x", "core"))
    over_mesh, over_panel = ("y", "z_lo"), ("z_hi", "x", "core")
    placed = (
        P(over_mesh, over_panel, None),
        P(over_mesh, None, None),
        P(over_mesh),
        P(over_mesh),
        P(over_mesh),
        P(over_mesh),
        P(over_mesh),
    )
    return jax.shard_map(
        local, mesh=fine, in_specs=placed, out_specs=P(over_panel, over_mesh), check_vma=False
    )
```

```python
import jax
import jax.numpy as jnp
import numpy as np
from jax import lax
from jax.experimental import pallas as pl
from jax.experimental.pallas import tpu as pltpu
from jax.sharding import Mesh
from jax.sharding import PartitionSpec as P

GMAX = 4
NEIGH = 4
DOFS = 192
OWN = 8
WIDTH = 64
CAP = 56
CHUNK = 4
PACKED = OWN * DOFS

neighbour_offsets = (1, -1, 2, -2)
ROW_STEP, COLUMN_STEP = 1, 3
VMEM = pl.BlockSpec(memory_space=pltpu.VMEM)
SMEM = pl.BlockSpec(memory_space=pltpu.SMEM)
HBM = pl.BlockSpec(memory_space=pltpu.HBM)


def pack_pair(first, second, out_ref, at):
    dtype = out_ref.dtype
    out_ref[:, at : at + 128] = first[:, :128].astype(dtype)
    out_ref[:, at + 128 : at + 256] = second[:, :128].astype(dtype)
    rest = jnp.concatenate([first[:, 128:], second[:, 128:]], axis=1)
    out_ref[:, at + 256 : at + 384] = rest.astype(dtype)


def select_kernel(send_ref, basis_ref, packed_ref, *ghost_refs):
    for neighbour, ghost_ref in enumerate(ghost_refs):
        for pair in range(GMAX // 2):
            at = neighbour * GMAX + 2 * pair
            pack_pair(
                basis_ref[send_ref[at]], basis_ref[send_ref[at + 1]], ghost_ref, 384 * pair
            )
    for pair in range(OWN // 2):
        pack_pair(basis_ref[2 * pair], basis_ref[2 * pair + 1], packed_ref, 384 * pair)


def block_kernel(
    rows_hbm, columns_hbm, density_hbm, count_hbm, basis_hbm, blocks_hbm, own_hbm, other_hbm, *rest
):
    ghost_refs = rest[:NEIGH]
    out_ref, pair_hbm, rows_ref, columns_ref, density_ref, count_ref, *rest = rest[NEIGH:]
    blocks, pool, total, arrived, lists, joined = rest
    small = [
        pltpu.make_async_copy(source, target, lists.at[index])
        for index, (source, target) in enumerate((
            (rows_hbm, rows_ref),
            (columns_hbm, columns_ref),
            (density_hbm, density_ref),
            (count_hbm, count_ref),
            (basis_hbm, pool.at[pl.ds(0, OWN)]),
        ))
    ]
    for copy in small:
        copy.start()
    copies = []
    for chunk in range(CAP // CHUNK):
        part = pl.ds(chunk * CHUNK, CHUNK)
        copies.append(
            pltpu.make_async_copy(blocks_hbm.at[part], blocks.at[part], arrived.at[chunk])
        )
        copies[-1].start()
    joins = [
        pltpu.make_async_copy(source, pair_hbm.at[pl.ds(index * WIDTH, WIDTH)], joined.at[index])
        for index, source in enumerate((own_hbm, other_hbm))
    ]
    for copy in joins:
        copy.start()
    for neighbour, ghost_ref in enumerate(ghost_refs):
        for pair in range(GMAX // 2):
            at, slot = 384 * pair, OWN + neighbour * GMAX + 2 * pair
            pool[slot, :, :128] = ghost_ref[:, at : at + 128]
            pool[slot + 1, :, :128] = ghost_ref[:, at + 128 : at + 256]
            pool[slot, :, 128:] = ghost_ref[:, at + 256 : at + 320]
            pool[slot + 1, :, 128:] = ghost_ref[:, at + 320 : at + 384]
    total[...] = jnp.zeros_like(total)
    for copy in small:
        copy.wait()
    count = count_ref[0]
    for chunk in range(CAP // CHUNK):
        copies[chunk].wait()
        for block in range(chunk * CHUNK, (chunk + 1) * CHUNK):
            density = density_ref[block]
            scale = jnp.where(block < count, 0.001 + density * density * density, 0.0)
            product = lax.dot_general(
                pool[columns_ref[block]],
                blocks[block],
                (((1,), (1,)), ((), ())),
                preferred_element_type=jnp.float32,
            )
            row = rows_ref[block]
            total[row] = total[row] + scale * product
    for pair in range(OWN // 2):
        pack_pair(total[2 * pair], total[2 * pair + 1], out_ref, 384 * pair)
    for copy in joins:
        copy.wait()


def put_tile(place_ref, products_ref, rows_ref, out_ref, z_step, column_step, row_step):
    half, x, core = place_ref[0], place_ref[1], place_ref[2]
    low_lanes = lax.broadcasted_iota(jnp.int32, (16, 2 * WIDTH), 1) < WIDTH
    tile = lax.dot_general(
        products_ref[...],
        rows_ref[...],
        (((1,), (1,)), ((), ())),
        preferred_element_type=jnp.float32,
    )
    for h in range(2):
        low, high = tile[32 * h : 32 * h + 16], tile[32 * h + 16 : 32 * h + 32]
        low_turned = pltpu.roll(low, WIDTH, 1)
        high_turned = pltpu.roll(high, WIDTH, 1)
        at = 16 * (half ^ z_step) + 4 * (x ^ (row_step ^ column_step)) + h
        out_ref[at + 2 * core] = jnp.where(low_lanes, low, high_turned)
        out_ref[at + 2 - 2 * core] = jnp.where(low_lanes, low_turned, high)


def own_tile_kernel(place_ref, pair_ref, products_ref, out_ref, pair_out_ref, products_out_ref):
    pair_out_ref[...] = pair_ref[...]
    products_out_ref[...] = products_ref[...]
    put_tile(place_ref, products_ref, pair_ref, out_ref, 0, 0, 0)


def tile_kernel(place_ref, pair_ref, other_pair_ref, *rest):
    *product_refs, begun_ref, out_ref = rest
    steps = ((0, 0), (1, 0), (0, COLUMN_STEP), (1, COLUMN_STEP))
    for (z_step, column_step), products_ref in zip(steps, product_refs):
        for row_step, rows_ref in ((0, pair_ref), (ROW_STEP, other_pair_ref)):
            if z_step or column_step or row_step:
                put_tile(
                    place_ref, products_ref, rows_ref, out_ref, z_step, column_step, row_step
                )


def sum_kernel(parts_ref, out_ref):
    total = jnp.sum(parts_ref[...].astype(jnp.float32), axis=0)
    out_ref[:16] = total[:, :WIDTH]
    out_ref[16:] = total[:, WIDTH:]


def local(
    basis_vectors, stiffness_blocks, block_rows, block_columns, density, block_counts, send_list
):
    mesh_axes, whole = ("y", "z_lo"), ("y", "z_lo", "z_hi", "x", "core")
    parts = lax.axis_size(mesh_axes)
    shape = jax.ShapeDtypeStruct
    packed, *picked = pl.pallas_call(
        select_kernel,
        out_shape=[shape((WIDTH, PACKED), jnp.bfloat16)]
        + [shape((WIDTH, GMAX * DOFS), jnp.bfloat16)] * NEIGH,
        in_specs=[SMEM, VMEM],
        out_specs=[VMEM] * (1 + NEIGH),
        name="select",
    )(send_list, basis_vectors)
    arriving = []
    for block, offset in zip(picked, neighbour_offsets):
        route = [((i - offset) % parts, i) for i in range(parts)]
        arriving.append(lax.ppermute(block, mesh_axes, route))
    swap = [(0, 1), (1, 0)]
    other_packed = lax.ppermute(packed, "core", swap)
    products, pair = pl.pallas_call(
        block_kernel,
        out_shape=[
            shape((WIDTH, PACKED), jnp.bfloat16),
            shape((2 * WIDTH, PACKED), jnp.bfloat16),
        ],
        in_specs=[HBM] * 8 + [VMEM] * NEIGH,
        out_specs=[VMEM, HBM],
        scratch_shapes=[
            pltpu.SMEM((CAP,), jnp.int32),
            pltpu.SMEM((CAP,), jnp.int32),
            pltpu.SMEM((CAP,), jnp.float32),
            pltpu.SMEM((1,), jnp.int32),
            pltpu.VMEM((CAP, DOFS, DOFS), jnp.bfloat16),
            pltpu.VMEM((OWN + NEIGH * GMAX, WIDTH, DOFS), jnp.bfloat16),
            pltpu.VMEM((OWN, WIDTH, DOFS), jnp.float32),
            pltpu.SemaphoreType.DMA((CAP // CHUNK,)),
            pltpu.SemaphoreType.DMA((5,)),
            pltpu.SemaphoreType.DMA((2,)),
        ],
        compiler_params=pltpu.CompilerParams(vmem_limit_bytes=64 << 20),
        name="blocks",
    )(
        block_rows,
        block_columns,
        density,
        block_counts,
        basis_vectors,
        stiffness_blocks,
        packed,
        other_packed,
        *arriving,
    )
    over_z = lax.ppermute(products, "z_hi", swap)
    over_x = lax.ppermute(products, "x", [(i, i ^ COLUMN_STEP) for i in range(4)])
    over_both = lax.ppermute(over_z, "x", [(i, i ^ COLUMN_STEP) for i in range(4)])
    other_pair = lax.ppermute(pair, "x", [(i, i ^ ROW_STEP) for i in range(4)])
    place = jnp.stack([lax.axis_index(name) for name in ("z_hi", "x", "core")]).astype(jnp.int32)
    chunks_shape = shape((parts, 16, 128), jnp.float32)
    begun, pair, products = pl.pallas_call(
        own_tile_kernel,
        out_shape=[
            chunks_shape,
            shape(pair.shape, pair.dtype),
            shape(products.shape, products.dtype),
        ],
        in_specs=[SMEM] + [VMEM] * 2,
        out_specs=[VMEM] * 3,
        compiler_params=pltpu.CompilerParams(vmem_limit_bytes=16 << 20),
        cost_estimate=pl.CostEstimate(flops=2 << 23, bytes_accessed=1 << 20, transcendentals=0),
        name="own_tile",
    )(place, pair, products)
    chunks = pl.pallas_call(
        tile_kernel,
        out_shape=chunks_shape,
        in_specs=[SMEM] + [VMEM] * 7,
        out_specs=VMEM,
        input_output_aliases={7: 0},
        compiler_params=pltpu.CompilerParams(vmem_limit_bytes=16 << 20),
        name="tile",
    )(place, pair, other_pair, products, over_z, over_x, over_both, begun)
    shares = lax.all_to_all(chunks, mesh_axes, 0, 0, tiled=True)
    block = pl.pallas_call(
        sum_kernel,
        out_shape=shape((32, WIDTH), jnp.float32),
        in_specs=[VMEM],
        out_specs=VMEM,
        compiler_params=pltpu.CompilerParams(vmem_limit_bytes=8 << 20),
        name="sum",
    )(shares)
    route = []
    for place in range(512):
        z2, x, u, v, c2, h, z, c = np.unravel_index(place, (2, 4, 2, 2, 2, 2, 2, 2))
        u, v = u * ROW_STEP, v * COLUMN_STEP
        source = (z2 * 16 + (x ^ u ^ v) * 4 + c2 * 2 + h) * 16 + z * 8 + x * 2 + c
        target = (z2 * 16 + (x ^ v) * 4 + c * 2 + h) * 16 + z * 8 + (x ^ u) * 2 + c2
        route.append((int(source), int(target)))
    return lax.ppermute(block, whole, route).T


def solution(mesh):
    fine = Mesh(mesh.devices.reshape(8, 4, 2, 4, 2), ("y", "z_lo", "z_hi", "x", "core"))
    over_mesh, over_panel = ("y", "z_lo"), ("z_hi", "x", "core")
    placed = (
        P(over_mesh, over_panel, None),
        P(over_mesh, None, None),
        P(over_mesh),
        P(over_mesh),
        P(over_mesh),
        P(over_mesh),
        P(over_mesh),
    )
    return jax.shard_map(
        local, mesh=fine, in_specs=placed, out_specs=P(over_panel, over_mesh), check_vma=False
    )
```

```python
import jax
import jax.numpy as jnp
import numpy as np
from jax import lax
from jax.experimental import pallas as pl
from jax.experimental.pallas import tpu as pltpu
from jax.sharding import Mesh
from jax.sharding import PartitionSpec as P

GMAX = 4
NEIGH = 4
DOFS = 192
OWN = 8
WIDTH = 64
CAP = 56
CHUNK = 4
PACKED = OWN * DOFS

neighbour_offsets = (1, -1, 2, -2)
NEAR, FAR = 1, 3
VMEM = pl.BlockSpec(memory_space=pltpu.VMEM)
SMEM = pl.BlockSpec(memory_space=pltpu.SMEM)
HBM = pl.BlockSpec(memory_space=pltpu.HBM)


def pack_pair(first, second, out_ref, at):
    dtype = out_ref.dtype
    out_ref[:, at : at + 128] = first[:, :128].astype(dtype)
    out_ref[:, at + 128 : at + 256] = second[:, :128].astype(dtype)
    rest = jnp.concatenate([first[:, 128:], second[:, 128:]], axis=1)
    out_ref[:, at + 256 : at + 384] = rest.astype(dtype)


def select_kernel(send_ref, basis_ref, packed_ref, *ghost_refs):
    for neighbour, ghost_ref in enumerate(ghost_refs):
        for pair in range(GMAX // 2):
            at = neighbour * GMAX + 2 * pair
            pack_pair(
                basis_ref[send_ref[at]], basis_ref[send_ref[at + 1]], ghost_ref, 384 * pair
            )
    for pair in range(OWN // 2):
        pack_pair(basis_ref[2 * pair], basis_ref[2 * pair + 1], packed_ref, 384 * pair)


def block_kernel(
    rows_hbm, columns_hbm, density_hbm, count_hbm, basis_hbm, blocks_hbm, own_hbm, other_hbm, *rest
):
    ghost_refs = rest[:NEIGH]
    out_ref, pair_ref, rows_ref, columns_ref, density_ref, count_ref, *rest = rest[NEIGH:]
    blocks, pool, total, arrived, lists, joined = rest
    small = [
        pltpu.make_async_copy(source, target, lists.at[index])
        for index, (source, target) in enumerate((
            (rows_hbm, rows_ref),
            (columns_hbm, columns_ref),
            (density_hbm, density_ref),
            (count_hbm, count_ref),
            (basis_hbm, pool.at[pl.ds(0, OWN)]),
        ))
    ]
    for copy in small:
        copy.start()
    copies = []
    for chunk in range(CAP // CHUNK):
        part = pl.ds(chunk * CHUNK, CHUNK)
        copies.append(
            pltpu.make_async_copy(blocks_hbm.at[part], blocks.at[part], arrived.at[chunk])
        )
        copies[-1].start()
    joins = [
        pltpu.make_async_copy(source, pair_ref.at[pl.ds(index * WIDTH, WIDTH)], joined.at[index])
        for index, source in enumerate((own_hbm, other_hbm))
    ]
    for copy in joins:
        copy.start()
    for neighbour, ghost_ref in enumerate(ghost_refs):
        for pair in range(GMAX // 2):
            at, slot = 384 * pair, OWN + neighbour * GMAX + 2 * pair
            pool[slot, :, :128] = ghost_ref[:, at : at + 128]
            pool[slot + 1, :, :128] = ghost_ref[:, at + 128 : at + 256]
            pool[slot, :, 128:] = ghost_ref[:, at + 256 : at + 320]
            pool[slot + 1, :, 128:] = ghost_ref[:, at + 320 : at + 384]
    total[...] = jnp.zeros_like(total)
    for copy in small:
        copy.wait()
    count = count_ref[0]
    for chunk in range(CAP // CHUNK):
        copies[chunk].wait()
        for block in range(chunk * CHUNK, (chunk + 1) * CHUNK):
            density = density_ref[block]
            scale = jnp.where(block < count, 0.001 + density * density * density, 0.0)
            product = lax.dot_general(
                pool[columns_ref[block]],
                blocks[block],
                (((1,), (1,)), ((), ())),
                preferred_element_type=jnp.float32,
            )
            row = rows_ref[block]
            total[row] = total[row] + scale * product
    for pair in range(OWN // 2):
        pack_pair(total[2 * pair], total[2 * pair + 1], out_ref, 384 * pair)
    for copy in joins:
        copy.wait()


def put_tile(place_ref, products_ref, rows_ref, out_ref, z_step, core_step, row_step):
    half, x, core = place_ref[0] ^ z_step, place_ref[1] ^ row_step, place_ref[2] ^ core_step
    low_lanes = lax.broadcasted_iota(jnp.int32, (16, 2 * WIDTH), 1) < WIDTH
    tile = lax.dot_general(
        products_ref[...],
        rows_ref[...],
        (((1,), (1,)), ((), ())),
        preferred_element_type=jnp.float32,
    )
    for h in range(2):
        low, high = tile[32 * h : 32 * h + 16], tile[32 * h + 16 : 32 * h + 32]
        low_turned = pltpu.roll(low, WIDTH, 1)
        high_turned = pltpu.roll(high, WIDTH, 1)
        at = 16 * half + 2 * core + h
        out_ref[at + 4 * x] = jnp.where(low_lanes, low, high_turned)
        out_ref[at + 4 * (x ^ NEAR)] = jnp.where(low_lanes, low_turned, high)


def own_tile_kernel(place_ref, pair_ref, products_ref, out_ref, pair_out_ref, products_out_ref):
    pair_out_ref[...] = pair_ref[...]
    products_out_ref[...] = products_ref[...]
    put_tile(place_ref, products_ref, pair_ref, out_ref, 0, 0, 0)


def tile_kernel(place_ref, pair_ref, other_pair_ref, *rest):
    *product_refs, begun_ref, out_ref = rest
    for (z_step, core_step), products_ref in zip(((0, 0), (0, 1), (1, 0), (1, 1)), product_refs):
        for row_step, rows_ref in ((0, pair_ref), (FAR, other_pair_ref)):
            if z_step or core_step or row_step:
                put_tile(
                    place_ref, products_ref, rows_ref, out_ref, z_step, core_step, row_step
                )


def sum_kernel(parts_ref, out_ref):
    total = jnp.sum(parts_ref[...].astype(jnp.float32), axis=0)
    out_ref[:16] = total[:, :WIDTH]
    out_ref[16:] = total[:, WIDTH:]


def local(
    basis_vectors, stiffness_blocks, block_rows, block_columns, density, block_counts, send_list
):
    mesh_axes, whole = ("y", "z_lo"), ("y", "z_lo", "z_hi", "x", "core")
    parts = lax.axis_size(mesh_axes)
    shape = jax.ShapeDtypeStruct
    packed, *picked = pl.pallas_call(
        select_kernel,
        out_shape=[shape((WIDTH, PACKED), jnp.bfloat16)]
        + [shape((WIDTH, GMAX * DOFS), jnp.bfloat16)] * NEIGH,
        in_specs=[SMEM, VMEM],
        out_specs=[VMEM] * (1 + NEIGH),
        name="select",
    )(send_list, basis_vectors)
    arriving = []
    for block, offset in zip(picked, neighbour_offsets):
        route = [((i - offset) % parts, i) for i in range(parts)]
        arriving.append(lax.ppermute(block, mesh_axes, route))
    swap = [(0, 1), (1, 0)]
    other_packed = lax.ppermute(packed, "x", [(i, i ^ NEAR) for i in range(4)])
    products, pair = pl.pallas_call(
        block_kernel,
        out_shape=[
            shape((WIDTH, PACKED), jnp.bfloat16),
            shape((2 * WIDTH, PACKED), jnp.bfloat16),
        ],
        in_specs=[HBM] * 8 + [VMEM] * NEIGH,
        out_specs=[VMEM] * 2,
        scratch_shapes=[
            pltpu.SMEM((CAP,), jnp.int32),
            pltpu.SMEM((CAP,), jnp.int32),
            pltpu.SMEM((CAP,), jnp.float32),
            pltpu.SMEM((1,), jnp.int32),
            pltpu.VMEM((CAP, DOFS, DOFS), jnp.bfloat16),
            pltpu.VMEM((OWN + NEIGH * GMAX, WIDTH, DOFS), jnp.bfloat16),
            pltpu.VMEM((OWN, WIDTH, DOFS), jnp.float32),
            pltpu.SemaphoreType.DMA((CAP // CHUNK,)),
            pltpu.SemaphoreType.DMA((5,)),
            pltpu.SemaphoreType.DMA((2,)),
        ],
        compiler_params=pltpu.CompilerParams(vmem_limit_bytes=64 << 20),
        name="blocks",
    )(
        block_rows,
        block_columns,
        density,
        block_counts,
        basis_vectors,
        stiffness_blocks,
        packed,
        other_packed,
        *arriving,
    )
    over_z = lax.ppermute(products, "z_hi", swap)
    over_core = lax.ppermute(products, "core", swap)
    other_pair = lax.ppermute(pair, "x", [(i, i ^ FAR) for i in range(4)])
    place = jnp.stack([lax.axis_index(name) for name in ("z_hi", "x", "core")]).astype(jnp.int32)
    chunks_shape = shape((parts, 16, 128), jnp.float32)
    begun, pair, products = pl.pallas_call(
        own_tile_kernel,
        out_shape=[
            chunks_shape,
            shape(pair.shape, pair.dtype),
            shape(products.shape, products.dtype),
        ],
        in_specs=[SMEM] + [VMEM] * 2,
        out_specs=[VMEM] * 3,
        compiler_params=pltpu.CompilerParams(vmem_limit_bytes=16 << 20),
        cost_estimate=pl.CostEstimate(flops=2 << 23, bytes_accessed=1 << 20, transcendentals=0),
        name="own_tile",
    )(place, pair, products)
    behind, begun = lax.optimization_barrier((over_z, begun))
    over_both = lax.ppermute(behind, "core", swap)
    chunks = pl.pallas_call(
        tile_kernel,
        out_shape=chunks_shape,
        in_specs=[SMEM] + [VMEM] * 7,
        out_specs=VMEM,
        input_output_aliases={7: 0},
        compiler_params=pltpu.CompilerParams(vmem_limit_bytes=16 << 20),
        name="tile",
    )(place, pair, other_pair, products, over_core, over_z, over_both, begun)
    shares = lax.all_to_all(chunks, mesh_axes, 0, 0, tiled=True)
    block = pl.pallas_call(
        sum_kernel,
        out_shape=shape((32, WIDTH), jnp.float32),
        in_specs=[VMEM],
        out_specs=VMEM,
        compiler_params=pltpu.CompilerParams(vmem_limit_bytes=8 << 20),
        name="sum",
    )(shares)
    route = []
    for place in range(512):
        z2, a, c2, h, z, b, c = (int(i) for i in np.unravel_index(place, (2, 4, 2, 2, 2, 4, 2)))
        source = (z2 * 16 + a * 4 + c2 * 2 + h) * 16 + z * 8 + b * 2 + c
        target = (z2 * 16 + b * 4 + c2 * 2 + h) * 16 + z * 8 + a * 2 + c
        route.append((source, target))
    return lax.ppermute(block, whole, route).T


def solution(mesh):
    fine = Mesh(mesh.devices.reshape(8, 4, 2, 4, 2), ("y", "z_lo", "z_hi", "x", "core"))
    over_mesh, over_panel = ("y", "z_lo"), ("z_hi", "x", "core")
    placed = (
        P(over_mesh, over_panel, None),
        P(over_mesh, None, None),
        P(over_mesh),
        P(over_mesh),
        P(over_mesh),
        P(over_mesh),
        P(over_mesh),
    )
    return jax.shard_map(
        local, mesh=fine, in_specs=placed, out_specs=P(over_panel, over_mesh), check_vma=False
    )
```

```python
import jax
import jax.numpy as jnp
import numpy as np
from jax import lax
from jax.experimental import pallas as pl
from jax.experimental.pallas import tpu as pltpu
from jax.sharding import Mesh
from jax.sharding import PartitionSpec as P

GMAX = 4
NEIGH = 4
DOFS = 192
OWN = 8
WIDTH = 64
CAP = 56
CHUNK = 4
PACKED = OWN * DOFS

neighbour_offsets = (1, -1, 2, -2)
NEAR, FAR = 1, 3
VMEM = pl.BlockSpec(memory_space=pltpu.VMEM)
SMEM = pl.BlockSpec(memory_space=pltpu.SMEM)
HBM = pl.BlockSpec(memory_space=pltpu.HBM)


def pack_pair(first, second, out_ref, at):
    dtype = out_ref.dtype
    out_ref[:, at : at + 128] = first[:, :128].astype(dtype)
    out_ref[:, at + 128 : at + 256] = second[:, :128].astype(dtype)
    rest = jnp.concatenate([first[:, 128:], second[:, 128:]], axis=1)
    out_ref[:, at + 256 : at + 384] = rest.astype(dtype)


def select_kernel(send_ref, basis_ref, packed_ref, *ghost_refs):
    for neighbour, ghost_ref in enumerate(ghost_refs):
        for pair in range(GMAX // 2):
            at = neighbour * GMAX + 2 * pair
            pack_pair(
                basis_ref[send_ref[at]], basis_ref[send_ref[at + 1]], ghost_ref, 384 * pair
            )
    for pair in range(OWN // 2):
        pack_pair(basis_ref[2 * pair], basis_ref[2 * pair + 1], packed_ref, 384 * pair)


def block_kernel(
    rows_hbm, columns_hbm, density_hbm, count_hbm, basis_hbm, blocks_hbm, own_hbm, other_hbm, *rest
):
    ghost_refs = rest[:NEIGH]
    out_ref, pair_ref, rows_ref, columns_ref, density_ref, count_ref, *rest = rest[NEIGH:]
    blocks, pool, total, arrived, lists, joined = rest
    small = [
        pltpu.make_async_copy(source, target, lists.at[index])
        for index, (source, target) in enumerate((
            (rows_hbm, rows_ref),
            (columns_hbm, columns_ref),
            (density_hbm, density_ref),
            (count_hbm, count_ref),
            (basis_hbm, pool.at[pl.ds(0, OWN)]),
        ))
    ]
    for copy in small:
        copy.start()
    copies = []
    for chunk in range(CAP // CHUNK):
        part = pl.ds(chunk * CHUNK, CHUNK)
        copies.append(
            pltpu.make_async_copy(blocks_hbm.at[part], blocks.at[part], arrived.at[chunk])
        )
        copies[-1].start()
    joins = [
        pltpu.make_async_copy(source, pair_ref.at[pl.ds(index * WIDTH, WIDTH)], joined.at[index])
        for index, source in enumerate((own_hbm, other_hbm))
    ]
    for copy in joins:
        copy.start()
    for neighbour, ghost_ref in enumerate(ghost_refs):
        for pair in range(GMAX // 2):
            at, slot = 384 * pair, OWN + neighbour * GMAX + 2 * pair
            pool[slot, :, :128] = ghost_ref[:, at : at + 128]
            pool[slot + 1, :, :128] = ghost_ref[:, at + 128 : at + 256]
            pool[slot, :, 128:] = ghost_ref[:, at + 256 : at + 320]
            pool[slot + 1, :, 128:] = ghost_ref[:, at + 320 : at + 384]
    total[...] = jnp.zeros_like(total)
    for copy in small:
        copy.wait()
    count = count_ref[0]
    for chunk in range(CAP // CHUNK):
        copies[chunk].wait()
        for block in range(chunk * CHUNK, (chunk + 1) * CHUNK):
            density = density_ref[block]
            scale = jnp.where(block < count, 0.001 + density * density * density, 0.0)
            product = lax.dot_general(
                pool[columns_ref[block]],
                blocks[block],
                (((1,), (1,)), ((), ())),
                preferred_element_type=jnp.float32,
            )
            row = rows_ref[block]
            total[row] = total[row] + scale * product
    for pair in range(OWN // 2):
        pack_pair(total[2 * pair], total[2 * pair + 1], out_ref, 384 * pair)
    for copy in joins:
        copy.wait()


def put_tile(place_ref, products_ref, rows_ref, out_ref, z_step, core_step, row_step):
    half, x, core = place_ref[0] ^ z_step, place_ref[1] ^ row_step, place_ref[2] ^ core_step
    low_lanes = lax.broadcasted_iota(jnp.int32, (16, 2 * WIDTH), 1) < WIDTH
    tile = lax.dot_general(
        products_ref[...],
        rows_ref[...],
        (((1,), (1,)), ((), ())),
        preferred_element_type=jnp.float32,
    )
    for h in range(2):
        low, high = tile[32 * h : 32 * h + 16], tile[32 * h + 16 : 32 * h + 32]
        low_turned = pltpu.roll(low, WIDTH, 1)
        high_turned = pltpu.roll(high, WIDTH, 1)
        at = 16 * half + 2 * core + h
        out_ref[at + 4 * x] = jnp.where(low_lanes, low, high_turned).astype(out_ref.dtype)
        out_ref[at + 4 * (x ^ NEAR)] = jnp.where(low_lanes, low_turned, high).astype(out_ref.dtype)


def own_tile_kernel(place_ref, pair_ref, products_ref, out_ref, pair_out_ref, products_out_ref):
    pair_out_ref[...] = pair_ref[...]
    products_out_ref[...] = products_ref[...]
    put_tile(place_ref, products_ref, pair_ref, out_ref, 0, 0, 0)


def tile_kernel(place_ref, pair_ref, other_pair_ref, *rest):
    *product_refs, begun_ref, out_ref = rest
    for (z_step, core_step), products_ref in zip(((0, 0), (0, 1), (1, 0), (1, 1)), product_refs):
        for row_step, rows_ref in ((0, pair_ref), (FAR, other_pair_ref)):
            if z_step or core_step or row_step:
                put_tile(
                    place_ref, products_ref, rows_ref, out_ref, z_step, core_step, row_step
                )


def sum_kernel(parts_ref, out_ref):
    total = jnp.sum(parts_ref[...].astype(jnp.float32), axis=0)
    out_ref[:16] = total[:, :WIDTH]
    out_ref[16:] = total[:, WIDTH:]


def local(
    basis_vectors, stiffness_blocks, block_rows, block_columns, density, block_counts, send_list
):
    mesh_axes, whole = ("y", "z_lo"), ("y", "z_lo", "z_hi", "x", "core")
    parts = lax.axis_size(mesh_axes)
    shape = jax.ShapeDtypeStruct
    packed, *picked = pl.pallas_call(
        select_kernel,
        out_shape=[shape((WIDTH, PACKED), jnp.bfloat16)]
        + [shape((WIDTH, GMAX * DOFS), jnp.bfloat16)] * NEIGH,
        in_specs=[SMEM, VMEM],
        out_specs=[VMEM] * (1 + NEIGH),
        name="select",
    )(send_list, basis_vectors)
    arriving = []
    for block, offset in zip(picked, neighbour_offsets):
        route = [((i - offset) % parts, i) for i in range(parts)]
        arriving.append(lax.ppermute(block, mesh_axes, route))
    swap = [(0, 1), (1, 0)]
    other_packed = lax.ppermute(packed, "x", [(i, i ^ NEAR) for i in range(4)])
    products, pair = pl.pallas_call(
        block_kernel,
        out_shape=[
            shape((WIDTH, PACKED), jnp.bfloat16),
            shape((2 * WIDTH, PACKED), jnp.bfloat16),
        ],
        in_specs=[HBM] * 8 + [VMEM] * NEIGH,
        out_specs=[VMEM] * 2,
        scratch_shapes=[
            pltpu.SMEM((CAP,), jnp.int32),
            pltpu.SMEM((CAP,), jnp.int32),
            pltpu.SMEM((CAP,), jnp.float32),
            pltpu.SMEM((1,), jnp.int32),
            pltpu.VMEM((CAP, DOFS, DOFS), jnp.bfloat16),
            pltpu.VMEM((OWN + NEIGH * GMAX, WIDTH, DOFS), jnp.bfloat16),
            pltpu.VMEM((OWN, WIDTH, DOFS), jnp.float32),
            pltpu.SemaphoreType.DMA((CAP // CHUNK,)),
            pltpu.SemaphoreType.DMA((5,)),
            pltpu.SemaphoreType.DMA((2,)),
        ],
        compiler_params=pltpu.CompilerParams(vmem_limit_bytes=64 << 20),
        name="blocks",
    )(
        block_rows,
        block_columns,
        density,
        block_counts,
        basis_vectors,
        stiffness_blocks,
        packed,
        other_packed,
        *arriving,
    )
    over_z = lax.ppermute(products, "z_hi", swap)
    over_core = lax.ppermute(products, "core", swap)
    other_pair = lax.ppermute(pair, "x", [(i, i ^ FAR) for i in range(4)])
    place = jnp.stack([lax.axis_index(name) for name in ("z_hi", "x", "core")]).astype(jnp.int32)
    chunks_shape = shape((parts, 16, 128), jnp.bfloat16)
    begun, pair, products = pl.pallas_call(
        own_tile_kernel,
        out_shape=[
            chunks_shape,
            shape(pair.shape, pair.dtype),
            shape(products.shape, products.dtype),
        ],
        in_specs=[SMEM] + [VMEM] * 2,
        out_specs=[VMEM] * 3,
        compiler_params=pltpu.CompilerParams(vmem_limit_bytes=16 << 20),
        cost_estimate=pl.CostEstimate(flops=2 << 23, bytes_accessed=1 << 20, transcendentals=0),
        name="own_tile",
    )(place, pair, products)
    behind, begun = lax.optimization_barrier((over_z, begun))
    over_both = lax.ppermute(behind, "core", swap)
    chunks = pl.pallas_call(
        tile_kernel,
        out_shape=chunks_shape,
        in_specs=[SMEM] + [VMEM] * 7,
        out_specs=VMEM,
        input_output_aliases={7: 0},
        compiler_params=pltpu.CompilerParams(vmem_limit_bytes=16 << 20),
        name="tile",
    )(place, pair, other_pair, products, over_core, over_z, over_both, begun)
    shares = lax.all_to_all(chunks, mesh_axes, 0, 0, tiled=True)
    block = pl.pallas_call(
        sum_kernel,
        out_shape=shape((32, WIDTH), jnp.float32),
        in_specs=[VMEM],
        out_specs=VMEM,
        compiler_params=pltpu.CompilerParams(vmem_limit_bytes=8 << 20),
        name="sum",
    )(shares)
    route = []
    for place in range(512):
        z2, a, c2, h, z, b, c = (int(i) for i in np.unravel_index(place, (2, 4, 2, 2, 2, 4, 2)))
        source = (z2 * 16 + a * 4 + c2 * 2 + h) * 16 + z * 8 + b * 2 + c
        target = (z2 * 16 + b * 4 + c2 * 2 + h) * 16 + z * 8 + a * 2 + c
        route.append((source, target))
    return lax.ppermute(block, whole, route).T


def solution(mesh):
    fine = Mesh(mesh.devices.reshape(8, 4, 2, 4, 2), ("y", "z_lo", "z_hi", "x", "core"))
    over_mesh, over_panel = ("y", "z_lo"), ("z_hi", "x", "core")
    placed = (
        P(over_mesh, over_panel, None),
        P(over_mesh, None, None),
        P(over_mesh),
        P(over_mesh),
        P(over_mesh),
        P(over_mesh),
        P(over_mesh),
    )
    return jax.shard_map(
        local, mesh=fine, in_specs=placed, out_specs=P(over_panel, over_mesh), check_vma=False
    )
```

```python
import jax
import jax.numpy as jnp
from jax import lax
from jax.experimental import pallas as pl
from jax.experimental.pallas import tpu as pltpu
from jax.sharding import Mesh
from jax.sharding import PartitionSpec as P

GMAX = 4
NEIGH = 4
DOFS = 192
OWN = 8
WIDTH = 64
CAP = 56
CHUNK = 4
PACKED = OWN * DOFS

neighbour_offsets = (1, -1, 2, -2)
NEAR, FAR = 1, 2
VMEM = pl.BlockSpec(memory_space=pltpu.VMEM)
SMEM = pl.BlockSpec(memory_space=pltpu.SMEM)
HBM = pl.BlockSpec(memory_space=pltpu.HBM)


def pack_pair(first, second, out_ref, at):
    dtype = out_ref.dtype
    out_ref[:, at : at + 128] = first[:, :128].astype(dtype)
    out_ref[:, at + 128 : at + 256] = second[:, :128].astype(dtype)
    rest = jnp.concatenate([first[:, 128:], second[:, 128:]], axis=1)
    out_ref[:, at + 256 : at + 384] = rest.astype(dtype)


def select_kernel(send_ref, basis_ref, packed_ref, *ghost_refs):
    for neighbour, ghost_ref in enumerate(ghost_refs):
        for pair in range(GMAX // 2):
            at = neighbour * GMAX + 2 * pair
            pack_pair(
                basis_ref[send_ref[at]], basis_ref[send_ref[at + 1]], ghost_ref, 384 * pair
            )
    for pair in range(OWN // 2):
        pack_pair(basis_ref[2 * pair], basis_ref[2 * pair + 1], packed_ref, 384 * pair)


def block_kernel(
    rows_hbm, columns_hbm, density_hbm, count_hbm, basis_hbm, blocks_hbm, *rest
):
    ghost_refs = rest[:NEIGH]
    out_ref, rows_ref, columns_ref, density_ref, count_ref, *rest = rest[NEIGH:]
    blocks, pool, total, arrived, lists = rest
    small = [
        pltpu.make_async_copy(source, target, lists.at[index])
        for index, (source, target) in enumerate((
            (rows_hbm, rows_ref),
            (columns_hbm, columns_ref),
            (density_hbm, density_ref),
            (count_hbm, count_ref),
            (basis_hbm, pool.at[pl.ds(0, OWN)]),
        ))
    ]
    for copy in small:
        copy.start()
    copies = []
    for chunk in range(CAP // CHUNK):
        part = pl.ds(chunk * CHUNK, CHUNK)
        copies.append(
            pltpu.make_async_copy(blocks_hbm.at[part], blocks.at[part], arrived.at[chunk])
        )
        copies[-1].start()
    for neighbour, ghost_ref in enumerate(ghost_refs):
        for pair in range(GMAX // 2):
            at, slot = 384 * pair, OWN + neighbour * GMAX + 2 * pair
            pool[slot, :, :128] = ghost_ref[:, at : at + 128]
            pool[slot + 1, :, :128] = ghost_ref[:, at + 128 : at + 256]
            pool[slot, :, 128:] = ghost_ref[:, at + 256 : at + 320]
            pool[slot + 1, :, 128:] = ghost_ref[:, at + 320 : at + 384]
    total[...] = jnp.zeros_like(total)
    for copy in small:
        copy.wait()
    count = count_ref[0]
    for chunk in range(CAP // CHUNK):
        copies[chunk].wait()
        for block in range(chunk * CHUNK, (chunk + 1) * CHUNK):
            density = density_ref[block]
            scale = jnp.where(block < count, 0.001 + density * density * density, 0.0)
            product = lax.dot_general(
                pool[columns_ref[block]],
                blocks[block],
                (((1,), (1,)), ((), ())),
                preferred_element_type=jnp.float32,
            )
            row = rows_ref[block]
            total[row] = total[row] + scale * product
    for pair in range(OWN // 2):
        pack_pair(total[2 * pair], total[2 * pair + 1], out_ref, 384 * pair)


def put_tile(place_ref, products_ref, rows_ref, out_ref, z_step, core_step, row_step):
    half, x, core = place_ref[0] ^ z_step, place_ref[1] ^ row_step, place_ref[2] ^ core_step
    low_lanes = lax.broadcasted_iota(jnp.int32, (16, 2 * WIDTH), 1) < WIDTH
    tile = lax.dot_general(
        products_ref[...],
        rows_ref[...],
        (((1,), (1,)), ((), ())),
        preferred_element_type=jnp.float32,
    )
    for h in range(2):
        low, high = tile[32 * h : 32 * h + 16], tile[32 * h + 16 : 32 * h + 32]
        low_turned = pltpu.roll(low, WIDTH, 1)
        high_turned = pltpu.roll(high, WIDTH, 1)
        at = 16 * half + 2 * core + h
        out_ref[at + 4 * x] = jnp.where(low_lanes, low, high_turned).astype(out_ref.dtype)
        out_ref[at + 4 * (x ^ NEAR)] = jnp.where(low_lanes, low_turned, high).astype(out_ref.dtype)


def join_kernel(own_ref, other_ref, pair_ref):
    pair_ref[:WIDTH] = own_ref[...]
    pair_ref[WIDTH:] = other_ref[...]


def tile_kernel(place_ref, pair_ref, other_pair_ref, *rest):
    *product_refs, out_ref = rest
    for (z_step, core_step), products_ref in zip(((0, 0), (0, 1), (1, 0), (1, 1)), product_refs):
        for row_step, rows_ref in ((0, pair_ref), (FAR, other_pair_ref)):
            put_tile(place_ref, products_ref, rows_ref, out_ref, z_step, core_step, row_step)


def sum_kernel(parts_ref, out_ref):
    total = jnp.sum(parts_ref[...].astype(jnp.float32), axis=0)
    out_ref[:16] = total[:, :WIDTH]
    out_ref[16:] = total[:, WIDTH:]


def local(
    basis_vectors, stiffness_blocks, block_rows, block_columns, density, block_counts, send_list
):
    mesh_axes = ("y_high", "y_low", "z_low")
    parts = lax.axis_size(mesh_axes)
    shape = jax.ShapeDtypeStruct
    packed, *picked = pl.pallas_call(
        select_kernel,
        out_shape=[shape((WIDTH, PACKED), jnp.bfloat16)]
        + [shape((WIDTH, GMAX * DOFS), jnp.bfloat16)] * NEIGH,
        in_specs=[SMEM, VMEM],
        out_specs=[VMEM] * (1 + NEIGH),
        name="select",
    )(send_list, basis_vectors)
    arriving = []
    for block, offset in zip(picked, neighbour_offsets):
        route = [((i - offset) % parts, i) for i in range(parts)]
        arriving.append(lax.ppermute(block, mesh_axes, route))
    swap = [(0, 1), (1, 0)]
    other_packed = lax.ppermute(packed, "x", [(i, i ^ NEAR) for i in range(4)])
    pair = pl.pallas_call(
        join_kernel,
        out_shape=shape((2 * WIDTH, PACKED), jnp.bfloat16),
        in_specs=[VMEM] * 2,
        out_specs=VMEM,
        name="join",
    )(packed, other_packed)
    block_rows, pair = lax.optimization_barrier((block_rows, pair))
    products = pl.pallas_call(
        block_kernel,
        out_shape=shape((WIDTH, PACKED), jnp.bfloat16),
        in_specs=[HBM] * 6 + [VMEM] * NEIGH,
        out_specs=VMEM,
        scratch_shapes=[
            pltpu.SMEM((CAP,), jnp.int32),
            pltpu.SMEM((CAP,), jnp.int32),
            pltpu.SMEM((CAP,), jnp.float32),
            pltpu.SMEM((1,), jnp.int32),
            pltpu.VMEM((CAP, DOFS, DOFS), jnp.bfloat16),
            pltpu.VMEM((OWN + NEIGH * GMAX, WIDTH, DOFS), jnp.bfloat16),
            pltpu.VMEM((OWN, WIDTH, DOFS), jnp.float32),
            pltpu.SemaphoreType.DMA((CAP // CHUNK,)),
            pltpu.SemaphoreType.DMA((5,)),
        ],
        compiler_params=pltpu.CompilerParams(vmem_limit_bytes=64 << 20),
        name="blocks",
    )(
        block_rows,
        block_columns,
        density,
        block_counts,
        basis_vectors,
        stiffness_blocks,
        *arriving,
    )
    across = ("y_low", "z_high", "x")
    swap_low = [(4 * b + a, 4 * a + b) for a in range(4) for b in range(4)]
    both = [(8 * b + 4 * z + a, 8 * a + 4 * (1 - z) + b) for a in range(4) for b in range(4) for z in range(2)]
    over_z = lax.ppermute(products, across, both)
    over_x = lax.ppermute(products, ("y_low", "x"), swap_low)
    over_x_core = lax.ppermute(over_x, "core", swap)
    over_z_core = lax.ppermute(over_z, "core", swap)
    pair, _ = lax.optimization_barrier((pair, products))
    pairs = [
        lax.ppermute(
            pair,
            ("y_low", "x"),
            [(4 * b + a, 4 * (a ^ step) + b) for a in range(4) for b in range(4)],
        )
        for step in (0, FAR)
    ]
    place = jnp.stack([lax.axis_index(name) for name in ("z_high", "y_low", "core")])
    chunks = pl.pallas_call(
        tile_kernel,
        out_shape=shape((parts, 16, 128), jnp.bfloat16),
        in_specs=[SMEM] + [VMEM] * 6,
        out_specs=VMEM,
        compiler_params=pltpu.CompilerParams(vmem_limit_bytes=16 << 20),
        name="tile",
    )(place.astype(jnp.int32), *pairs, over_x, over_x_core, over_z, over_z_core)
    shares = lax.all_to_all(chunks, ("y_high", "x", "z_low"), 0, 0, tiled=True)
    block = pl.pallas_call(
        sum_kernel,
        out_shape=shape((32, WIDTH), jnp.float32),
        in_specs=[VMEM],
        out_specs=VMEM,
        compiler_params=pltpu.CompilerParams(vmem_limit_bytes=8 << 20),
        name="sum",
    )(shares)
    return block.T


def solution(mesh):
    names = ("y_high", "y_low", "z_low", "z_high", "x", "core")
    fine = Mesh(mesh.devices.reshape(2, 4, 4, 2, 4, 2), names)
    over_mesh, over_panel = names[:3], names[3:]
    placed = (
        P(over_mesh, over_panel, None),
        P(over_mesh, None, None),
        P(over_mesh),
        P(over_mesh),
        P(over_mesh),
        P(over_mesh),
        P(over_mesh),
    )
    return jax.shard_map(
        local, mesh=fine, in_specs=placed, out_specs=P(over_panel, over_mesh), check_vma=False
    )
```

```python
import jax
import jax.numpy as jnp
import numpy as np
from jax import lax
from jax.experimental import pallas as pl
from jax.experimental.pallas import tpu as pltpu
from jax.sharding import Mesh
from jax.sharding import PartitionSpec as P

GMAX = 4
NEIGH = 4
DOFS = 192
OWN = 8
WIDTH = 64
CAP = 56
PACKED = OWN * DOFS

neighbour_offsets = (1, -1, 2, -2)
NEAR, FAR = 1, 3
VMEM = pl.BlockSpec(memory_space=pltpu.VMEM)
SMEM = pl.BlockSpec(memory_space=pltpu.SMEM)
HBM = pl.BlockSpec(memory_space=pltpu.HBM)


def pack_pair(first, second, out_ref, at):
    dtype = out_ref.dtype
    out_ref[:, at : at + 128] = first[:, :128].astype(dtype)
    out_ref[:, at + 128 : at + 256] = second[:, :128].astype(dtype)
    rest = jnp.concatenate([first[:, 128:], second[:, 128:]], axis=1)
    out_ref[:, at + 256 : at + 384] = rest.astype(dtype)


def select_kernel(send_ref, basis_ref, packed_ref, *ghost_refs):
    for neighbour, ghost_ref in enumerate(ghost_refs):
        for pair in range(GMAX // 2):
            at = neighbour * GMAX + 2 * pair
            pack_pair(
                basis_ref[send_ref[at]], basis_ref[send_ref[at + 1]], ghost_ref, 384 * pair
            )
    for pair in range(OWN // 2):
        pack_pair(basis_ref[2 * pair], basis_ref[2 * pair + 1], packed_ref, 384 * pair)


def stage_kernel(blocks_ref, basis_ref, blocks_out_ref, own_ref):
    blocks_out_ref[...] = blocks_ref[...]
    own_ref[...] = basis_ref[...]


def join_kernel(own_ref, other_ref, pair_ref):
    pair_ref[:WIDTH] = own_ref[...]
    pair_ref[WIDTH:] = other_ref[...]


def block_kernel(table_ref, own_ref, blocks_ref, *rest):
    *ghost_refs, out_ref, pool, total = rest
    pool[:OWN] = own_ref[...]
    for neighbour, ghost_ref in enumerate(ghost_refs):
        for pair in range(GMAX // 2):
            at, slot = 384 * pair, OWN + neighbour * GMAX + 2 * pair
            pool[slot, :, :128] = ghost_ref[:, at : at + 128]
            pool[slot + 1, :, :128] = ghost_ref[:, at + 128 : at + 256]
            pool[slot, :, 128:] = ghost_ref[:, at + 256 : at + 320]
            pool[slot + 1, :, 128:] = ghost_ref[:, at + 320 : at + 384]
    total[...] = jnp.zeros_like(total)
    for block in range(CAP):
        row, column = table_ref[0, block].astype(jnp.int32), table_ref[1, block].astype(jnp.int32)
        product = lax.dot_general(
            pool[column],
            blocks_ref[block],
            (((1,), (1,)), ((), ())),
            preferred_element_type=jnp.float32,
        )
        total[row] = total[row] + table_ref[2, block] * product
    for pair in range(OWN // 2):
        pack_pair(total[2 * pair], total[2 * pair + 1], out_ref, 384 * pair)


def put_tile(place_ref, products_ref, rows_ref, out_ref, z_step, core_step, row_step):
    half, x, core = place_ref[0] ^ z_step, place_ref[1] ^ row_step, place_ref[2] ^ core_step
    low_lanes = lax.broadcasted_iota(jnp.int32, (16, 2 * WIDTH), 1) < WIDTH
    tile = lax.dot_general(
        products_ref[...],
        rows_ref[...],
        (((1,), (1,)), ((), ())),
        preferred_element_type=jnp.float32,
    )
    for h in range(2):
        low, high = tile[32 * h : 32 * h + 16], tile[32 * h + 16 : 32 * h + 32]
        low_turned = pltpu.roll(low, WIDTH, 1)
        high_turned = pltpu.roll(high, WIDTH, 1)
        at = 16 * half + 2 * core + h
        out_ref[at + 4 * x] = jnp.where(low_lanes, low, high_turned).astype(out_ref.dtype)
        out_ref[at + 4 * (x ^ NEAR)] = jnp.where(low_lanes, low_turned, high).astype(out_ref.dtype)


def own_tile_kernel(place_ref, pair_ref, products_ref, out_ref):
    put_tile(place_ref, products_ref, pair_ref, out_ref, 0, 0, 0)


def tile_kernel(place_ref, pair_ref, other_pair_ref, *rest):
    *product_refs, begun_ref, out_ref = rest
    for (z_step, core_step), products_ref in zip(((0, 0), (0, 1), (1, 0), (1, 1)), product_refs):
        for row_step, rows_ref in ((0, pair_ref), (FAR, other_pair_ref)):
            if z_step or core_step or row_step:
                put_tile(
                    place_ref, products_ref, rows_ref, out_ref, z_step, core_step, row_step
                )


def sum_kernel(parts_ref, out_ref):
    total = jnp.sum(parts_ref[...].astype(jnp.float32), axis=0)
    out_ref[:16] = total[:, :WIDTH]
    out_ref[16:] = total[:, WIDTH:]


def local(
    basis_vectors, stiffness_blocks, block_rows, block_columns, density, block_counts, send_list
):
    mesh_axes, whole = ("y", "z_lo"), ("y", "z_lo", "z_hi", "x", "core")
    parts = lax.axis_size(mesh_axes)
    shape = jax.ShapeDtypeStruct
    packed, *picked = pl.pallas_call(
        select_kernel,
        out_shape=[shape((WIDTH, PACKED), jnp.bfloat16)]
        + [shape((WIDTH, GMAX * DOFS), jnp.bfloat16)] * NEIGH,
        in_specs=[SMEM, VMEM],
        out_specs=[VMEM] * (1 + NEIGH),
        name="select",
    )(send_list, basis_vectors)
    arriving = []
    for block, offset in zip(picked, neighbour_offsets):
        route = [((i - offset) % parts, i) for i in range(parts)]
        arriving.append(lax.ppermute(block, mesh_axes, route))
    swap = [(0, 1), (1, 0)]
    blocks, own = pl.pallas_call(
        stage_kernel,
        out_shape=[
            shape(stiffness_blocks.shape, jnp.bfloat16),
            shape(basis_vectors.shape, jnp.bfloat16),
        ],
        in_specs=[VMEM] * 2,
        out_specs=[VMEM] * 2,
        compiler_params=pltpu.CompilerParams(vmem_limit_bytes=24 << 20),
        cost_estimate=pl.CostEstimate(flops=0, bytes_accessed=12 << 20, transcendentals=0),
        name="stage",
    )(stiffness_blocks, basis_vectors)
    active = jnp.arange(CAP, dtype=jnp.int32) < block_counts[0]
    scale = jnp.where(active, 0.001 + density * density * density, 0.0)
    line = lax.broadcasted_iota(jnp.int32, (8, CAP), 0)
    places = jnp.where(line == 0, block_rows[None], block_columns[None]).astype(jnp.float32)
    table = jnp.where(line == 2, scale[None], places)
    other_packed = lax.ppermute(packed, "x", [(i, i ^ NEAR) for i in range(4)])
    products = pl.pallas_call(
        block_kernel,
        out_shape=shape((WIDTH, PACKED), jnp.bfloat16),
        in_specs=[SMEM] + [VMEM] * (2 + NEIGH),
        out_specs=VMEM,
        scratch_shapes=[
            pltpu.VMEM((OWN + NEIGH * GMAX, WIDTH, DOFS), jnp.bfloat16),
            pltpu.VMEM((OWN, WIDTH, DOFS), jnp.float32),
        ],
        compiler_params=pltpu.CompilerParams(vmem_limit_bytes=24 << 20),
        name="blocks",
    )(table, own, blocks, *arriving)
    other_packed, _ = lax.optimization_barrier((other_packed, products))
    pair = pl.pallas_call(
        join_kernel,
        out_shape=shape((2 * WIDTH, PACKED), jnp.bfloat16),
        in_specs=[VMEM] * 2,
        out_specs=VMEM,
        compiler_params=pltpu.CompilerParams(vmem_limit_bytes=8 << 20),
        name="join",
    )(packed, other_packed)
    over_z = lax.ppermute(products, "z_hi", swap)
    over_core = lax.ppermute(products, "core", swap)
    other_pair = lax.ppermute(pair, "x", [(i, i ^ FAR) for i in range(4)])
    place = jnp.stack([lax.axis_index(name) for name in ("z_hi", "x", "core")]).astype(jnp.int32)
    chunks_shape = shape((parts, 16, 128), jnp.bfloat16)
    begun = pl.pallas_call(
        own_tile_kernel,
        out_shape=chunks_shape,
        in_specs=[SMEM] + [VMEM] * 2,
        out_specs=VMEM,
        compiler_params=pltpu.CompilerParams(vmem_limit_bytes=16 << 20),
        cost_estimate=pl.CostEstimate(flops=2 << 23, bytes_accessed=1 << 20, transcendentals=0),
        name="own_tile",
    )(place, pair, products)
    behind, begun = lax.optimization_barrier((over_z, begun))
    over_both = lax.ppermute(behind, "core", swap)
    chunks = pl.pallas_call(
        tile_kernel,
        out_shape=chunks_shape,
        in_specs=[SMEM] + [VMEM] * 7,
        out_specs=VMEM,
        input_output_aliases={7: 0},
        compiler_params=pltpu.CompilerParams(vmem_limit_bytes=16 << 20),
        name="tile",
    )(place, pair, other_pair, products, over_core, over_z, over_both, begun)
    shares = lax.all_to_all(chunks, mesh_axes, 0, 0, tiled=True)
    block = pl.pallas_call(
        sum_kernel,
        out_shape=shape((32, WIDTH), jnp.float32),
        in_specs=[VMEM],
        out_specs=VMEM,
        compiler_params=pltpu.CompilerParams(vmem_limit_bytes=8 << 20),
        name="sum",
    )(shares)
    route = []
    for place in range(512):
        z2, a, c2, h, z, b, c = (int(i) for i in np.unravel_index(place, (2, 4, 2, 2, 2, 4, 2)))
        source = (z2 * 16 + a * 4 + c2 * 2 + h) * 16 + z * 8 + b * 2 + c
        target = (z2 * 16 + b * 4 + c2 * 2 + h) * 16 + z * 8 + a * 2 + c
        route.append((source, target))
    return lax.ppermute(block, whole, route).T


def solution(mesh):
    fine = Mesh(mesh.devices.reshape(8, 4, 2, 4, 2), ("y", "z_lo", "z_hi", "x", "core"))
    over_mesh, over_panel = ("y", "z_lo"), ("z_hi", "x", "core")
    placed = (
        P(over_mesh, over_panel, None),
        P(over_mesh, None, None),
        P(over_mesh),
        P(over_mesh),
        P(over_mesh),
        P(over_mesh),
        P(over_mesh),
    )
    return jax.shard_map(
        local, mesh=fine, in_specs=placed, out_specs=P(over_panel, over_mesh), check_vma=False
    )
```

```python
import jax
import jax.numpy as jnp
import numpy as np
from jax import lax
from jax.experimental import pallas as pl
from jax.experimental.pallas import tpu as pltpu
from jax.sharding import Mesh
from jax.sharding import PartitionSpec as P

GMAX = 4
NEIGH = 4
DOFS = 192
OWN = 8
WIDTH = 64
CAP = 56
PACKED = OWN * DOFS

neighbour_offsets = (1, -1, 2, -2)
NEAR, FAR = 1, 3
VMEM = pl.BlockSpec(memory_space=pltpu.VMEM)
SMEM = pl.BlockSpec(memory_space=pltpu.SMEM)
HBM = pl.BlockSpec(memory_space=pltpu.HBM)


def pack_pair(first, second, out_ref, at):
    dtype = out_ref.dtype
    out_ref[:, at : at + 128] = first[:, :128].astype(dtype)
    out_ref[:, at + 128 : at + 256] = second[:, :128].astype(dtype)
    rest = jnp.concatenate([first[:, 128:], second[:, 128:]], axis=1)
    out_ref[:, at + 256 : at + 384] = rest.astype(dtype)


def select_kernel(send_ref, basis_ref, packed_ref, *ghost_refs):
    for neighbour, ghost_ref in enumerate(ghost_refs):
        for pair in range(GMAX // 2):
            at = neighbour * GMAX + 2 * pair
            pack_pair(
                basis_ref[send_ref[at]], basis_ref[send_ref[at + 1]], ghost_ref, 384 * pair
            )
    for pair in range(OWN // 2):
        pack_pair(basis_ref[2 * pair], basis_ref[2 * pair + 1], packed_ref, 384 * pair)


def stage_kernel(blocks_ref, packed_ref, blocks_out_ref, packed_out_ref):
    blocks_out_ref[...] = blocks_ref[...]
    packed_out_ref[...] = packed_ref[...]


def join_kernel(own_ref, other_ref, pair_ref):
    pair_ref[:WIDTH] = own_ref[...]
    pair_ref[WIDTH:] = other_ref[...]


def block_kernel(table_ref, own_ref, blocks_ref, *rest):
    *ghost_refs, out_ref, pool, total = rest
    slot = 0
    for slabs_ref in (own_ref, *ghost_refs):
        for at in range(0, slabs_ref.shape[1], 384):
            pool[slot, :, :128] = slabs_ref[:, at : at + 128]
            pool[slot + 1, :, :128] = slabs_ref[:, at + 128 : at + 256]
            pool[slot, :, 128:] = slabs_ref[:, at + 256 : at + 320]
            pool[slot + 1, :, 128:] = slabs_ref[:, at + 320 : at + 384]
            slot += 2
    total[...] = jnp.zeros_like(total)
    count = table_ref[2, 0].astype(jnp.int32)
    for block in range(CAP):
        row, column = table_ref[0, block].astype(jnp.int32), table_ref[1, block].astype(jnp.int32)
        product = lax.dot_general(
            pool[column],
            blocks_ref[block],
            (((1,), (1,)), ((), ())),
            preferred_element_type=jnp.float32,
        )
        density = table_ref[3, block]
        scale = jnp.where(block < count, 0.001 + density * density * density, 0.0)
        total[row] = total[row] + scale * product
    for pair in range(OWN // 2):
        pack_pair(total[2 * pair], total[2 * pair + 1], out_ref, 384 * pair)


def put_tile(place_ref, products, rows, out_ref, steps, row_step):
    low_lanes = lax.broadcasted_iota(jnp.int32, (16, 2 * WIDTH), 1) < WIDTH
    tile = lax.dot_general(
        products, rows, (((1,), (1,)), ((), ())), preferred_element_type=jnp.float32
    )
    x = place_ref[1] ^ row_step
    for index, (z_step, core_step) in enumerate(steps):
        half, core = place_ref[0] ^ z_step, place_ref[2] ^ core_step
        for h in range(2):
            at = WIDTH * index + 32 * h
            low, high = tile[at : at + 16], tile[at + 16 : at + 32]
            low_turned = pltpu.roll(low, WIDTH, 1)
            high_turned = pltpu.roll(high, WIDTH, 1)
            at = 16 * half + 2 * core + h
            first = jnp.where(low_lanes, low, high_turned)
            second = jnp.where(low_lanes, low_turned, high)
            out_ref[at + 4 * x] = first.astype(out_ref.dtype)
            out_ref[at + 4 * (x ^ NEAR)] = second.astype(out_ref.dtype)


def own_tile_kernel(place_ref, pair_ref, products_ref, out_ref):
    put_tile(place_ref, products_ref[...], pair_ref[...], out_ref, ((0, 0),), 0)


def tile_kernel(place_ref, pair_ref, other_pair_ref, *rest):
    *product_refs, begun_ref, out_ref = rest
    steps = ((0, 0), (0, 1), (1, 0), (1, 1))
    products = jnp.concatenate([ref[...] for ref in product_refs], axis=0)
    put_tile(place_ref, products, other_pair_ref[...], out_ref, steps, FAR)
    put_tile(place_ref, products[WIDTH:], pair_ref[...], out_ref, steps[1:], 0)


def sum_kernel(parts_ref, out_ref):
    total = jnp.sum(parts_ref[...].astype(jnp.float32), axis=0)
    out_ref[:16] = total[:, :WIDTH]
    out_ref[16:] = total[:, WIDTH:]


def local(
    basis_vectors, stiffness_blocks, block_rows, block_columns, density, block_counts, send_list
):
    mesh_axes, whole = ("y", "z_lo"), ("y", "z_lo", "z_hi", "x", "core")
    parts = lax.axis_size(mesh_axes)
    shape = jax.ShapeDtypeStruct
    packed, *picked = pl.pallas_call(
        select_kernel,
        out_shape=[shape((WIDTH, PACKED), jnp.bfloat16)]
        + [shape((WIDTH, GMAX * DOFS), jnp.bfloat16)] * NEIGH,
        in_specs=[SMEM, VMEM],
        out_specs=[VMEM] * (1 + NEIGH),
        name="select",
    )(send_list, basis_vectors)
    arriving = []
    for block, offset in zip(picked, neighbour_offsets):
        route = [((i - offset) % parts, i) for i in range(parts)]
        arriving.append(lax.ppermute(block, mesh_axes, route))
    swap = [(0, 1), (1, 0)]
    blocks, own = pl.pallas_call(
        stage_kernel,
        out_shape=[
            shape(stiffness_blocks.shape, jnp.bfloat16),
            shape((WIDTH, PACKED), jnp.bfloat16),
        ],
        in_specs=[VMEM] * 2,
        out_specs=[VMEM] * 2,
        compiler_params=pltpu.CompilerParams(vmem_limit_bytes=24 << 20),
        cost_estimate=pl.CostEstimate(flops=0, bytes_accessed=12 << 20, transcendentals=0),
        name="stage",
    )(stiffness_blocks, packed)
    line = lax.broadcasted_iota(jnp.int32, (8, CAP), 0)
    listed = jnp.where(line == 0, block_rows[None], block_columns[None])
    listed = jnp.where(line == 2, block_counts[0], listed).astype(jnp.float32)
    table = jnp.where(line == 3, density[None], listed)
    other_packed = lax.ppermute(packed, "x", [(i, i ^ NEAR) for i in range(4)])
    products = pl.pallas_call(
        block_kernel,
        out_shape=shape((WIDTH, PACKED), jnp.bfloat16),
        in_specs=[SMEM] + [VMEM] * (2 + NEIGH),
        out_specs=VMEM,
        scratch_shapes=[
            pltpu.VMEM((OWN + NEIGH * GMAX, WIDTH, DOFS), jnp.bfloat16),
            pltpu.VMEM((OWN, WIDTH, DOFS), jnp.float32),
        ],
        compiler_params=pltpu.CompilerParams(vmem_limit_bytes=24 << 20),
        name="blocks",
    )(table, own, blocks, *arriving)
    other_packed, _ = lax.optimization_barrier((other_packed, products))
    pair = pl.pallas_call(
        join_kernel,
        out_shape=shape((2 * WIDTH, PACKED), jnp.bfloat16),
        in_specs=[VMEM] * 2,
        out_specs=VMEM,
        compiler_params=pltpu.CompilerParams(vmem_limit_bytes=8 << 20),
        name="join",
    )(own, other_packed)
    over_z = lax.ppermute(products, "z_hi", swap)
    over_core = lax.ppermute(products, "core", swap)
    other_pair = lax.ppermute(pair, "x", [(i, i ^ FAR) for i in range(4)])
    place = jnp.stack([lax.axis_index(name) for name in ("z_hi", "x", "core")]).astype(jnp.int32)
    chunks_shape = shape((parts, 16, 128), jnp.bfloat16)
    begun = pl.pallas_call(
        own_tile_kernel,
        out_shape=chunks_shape,
        in_specs=[SMEM] + [VMEM] * 2,
        out_specs=VMEM,
        compiler_params=pltpu.CompilerParams(vmem_limit_bytes=16 << 20),
        cost_estimate=pl.CostEstimate(flops=2 << 23, bytes_accessed=1 << 20, transcendentals=0),
        name="own_tile",
    )(place, pair, products)
    behind, begun = lax.optimization_barrier((over_z, begun))
    over_both = lax.ppermute(behind, "core", swap)
    chunks = pl.pallas_call(
        tile_kernel,
        out_shape=chunks_shape,
        in_specs=[SMEM] + [VMEM] * 7,
        out_specs=VMEM,
        input_output_aliases={7: 0},
        compiler_params=pltpu.CompilerParams(vmem_limit_bytes=16 << 20),
        name="tile",
    )(place, pair, other_pair, products, over_core, over_z, over_both, begun)
    shares = lax.all_to_all(chunks, mesh_axes, 0, 0, tiled=True)
    block = pl.pallas_call(
        sum_kernel,
        out_shape=shape((32, WIDTH), jnp.float32),
        in_specs=[VMEM],
        out_specs=VMEM,
        compiler_params=pltpu.CompilerParams(vmem_limit_bytes=8 << 20),
        name="sum",
    )(shares)
    route = []
    for place in range(512):
        z2, a, c2, h, z, b, c = (int(i) for i in np.unravel_index(place, (2, 4, 2, 2, 2, 4, 2)))
        source = (z2 * 16 + a * 4 + c2 * 2 + h) * 16 + z * 8 + b * 2 + c
        target = (z2 * 16 + b * 4 + c2 * 2 + h) * 16 + z * 8 + a * 2 + c
        route.append((source, target))
    return lax.ppermute(block, whole, route).T


def solution(mesh):
    fine = Mesh(mesh.devices.reshape(8, 4, 2, 4, 2), ("y", "z_lo", "z_hi", "x", "core"))
    over_mesh, over_panel = ("y", "z_lo"), ("z_hi", "x", "core")
    placed = (
        P(over_mesh, over_panel, None),
        P(over_mesh, None, None),
        P(over_mesh),
        P(over_mesh),
        P(over_mesh),
        P(over_mesh),
        P(over_mesh),
    )
    return jax.shard_map(
        local, mesh=fine, in_specs=placed, out_specs=P(over_panel, over_mesh), check_vma=False
    )
```

```python
import jax
import jax.numpy as jnp
import numpy as np
from jax import lax
from jax.experimental import pallas as pl
from jax.experimental.pallas import tpu as pltpu
from jax.sharding import Mesh
from jax.sharding import PartitionSpec as P

GMAX = 4
NEIGH = 4
DOFS = 192
OWN = 8
WIDTH = 64
CAP = 56
PACKED = OWN * DOFS

neighbour_offsets = (1, -1, 2, -2)
NEAR, FAR = 1, 3
VMEM = pl.BlockSpec(memory_space=pltpu.VMEM)
SMEM = pl.BlockSpec(memory_space=pltpu.SMEM)
HBM = pl.BlockSpec(memory_space=pltpu.HBM)


def pack_pair(first, second, out_ref, at):
    dtype = out_ref.dtype
    out_ref[:, at : at + 128] = first[:, :128].astype(dtype)
    out_ref[:, at + 128 : at + 256] = second[:, :128].astype(dtype)
    rest = jnp.concatenate([first[:, 128:], second[:, 128:]], axis=1)
    out_ref[:, at + 256 : at + 384] = rest.astype(dtype)


def select_kernel(send_ref, basis_ref, packed_ref, *ghost_refs):
    for neighbour, ghost_ref in enumerate(ghost_refs):
        for pair in range(GMAX // 2):
            at = neighbour * GMAX + 2 * pair
            pack_pair(
                basis_ref[send_ref[at]], basis_ref[send_ref[at + 1]], ghost_ref, 384 * pair
            )
    for pair in range(OWN // 2):
        pack_pair(basis_ref[2 * pair], basis_ref[2 * pair + 1], packed_ref, 384 * pair)


def stage_kernel(blocks_ref, blocks_out_ref):
    blocks_out_ref[...] = blocks_ref[...]


def join_kernel(own_ref, other_ref, pair_ref):
    pair_ref[:WIDTH] = own_ref[...]
    pair_ref[WIDTH:] = other_ref[...]


def block_kernel(table_ref, own_ref, blocks_ref, *rest):
    *ghost_refs, out_ref, pool, total = rest
    slot = 0
    for slabs_ref in (own_ref, *ghost_refs):
        for at in range(0, slabs_ref.shape[1], 384):
            pool[slot, :, :128] = slabs_ref[:, at : at + 128]
            pool[slot + 1, :, :128] = slabs_ref[:, at + 128 : at + 256]
            pool[slot, :, 128:] = slabs_ref[:, at + 256 : at + 320]
            pool[slot + 1, :, 128:] = slabs_ref[:, at + 320 : at + 384]
            slot += 2
    total[...] = jnp.zeros_like(total)
    count = table_ref[2, 0].astype(jnp.int32)
    for block in range(CAP):
        row, column = table_ref[0, block].astype(jnp.int32), table_ref[1, block].astype(jnp.int32)
        product = lax.dot_general(
            pool[column],
            blocks_ref[block],
            (((1,), (1,)), ((), ())),
            preferred_element_type=jnp.float32,
        )
        density = table_ref[3, block]
        scale = jnp.where(block < count, 0.001 + density * density * density, 0.0)
        total[row] = total[row] + scale * product
    for pair in range(OWN // 2):
        pack_pair(total[2 * pair], total[2 * pair + 1], out_ref, 384 * pair)


def put_tile(place_ref, products, rows, out_ref, steps, row_step):
    low_lanes = lax.broadcasted_iota(jnp.int32, (16, 2 * WIDTH), 1) < WIDTH
    tile = lax.dot_general(
        products, rows, (((1,), (1,)), ((), ())), preferred_element_type=jnp.float32
    )
    x = place_ref[1] ^ row_step
    for index, (z_step, core_step) in enumerate(steps):
        half, core = place_ref[0] ^ z_step, place_ref[2] ^ core_step
        for h in range(2):
            at = WIDTH * index + 32 * h
            low, high = tile[at : at + 16], tile[at + 16 : at + 32]
            low_turned = pltpu.roll(low, WIDTH, 1)
            high_turned = pltpu.roll(high, WIDTH, 1)
            at = 16 * half + 2 * core + h
            first = jnp.where(low_lanes, low, high_turned)
            second = jnp.where(low_lanes, low_turned, high)
            out_ref[at + 4 * x] = first.astype(out_ref.dtype)
            out_ref[at + 4 * (x ^ NEAR)] = second.astype(out_ref.dtype)


def own_tile_kernel(place_ref, pair_ref, products_ref, out_ref):
    put_tile(place_ref, products_ref[...], pair_ref[...], out_ref, ((0, 0),), 0)


def tile_kernel(place_ref, pair_ref, other_pair_ref, *rest):
    *product_refs, begun_ref, out_ref = rest
    steps = ((0, 0), (0, 1), (1, 0), (1, 1))
    products = jnp.concatenate([ref[...] for ref in product_refs], axis=0)
    put_tile(place_ref, products, other_pair_ref[...], out_ref, steps, FAR)
    put_tile(place_ref, products[WIDTH:], pair_ref[...], out_ref, steps[1:], 0)


def sum_kernel(parts_ref, out_ref):
    total = jnp.sum(parts_ref[...].astype(jnp.float32), axis=0)
    out_ref[:16] = total[:, :WIDTH]
    out_ref[16:] = total[:, WIDTH:]


def local(
    basis_vectors, stiffness_blocks, block_rows, block_columns, density, block_counts, send_list
):
    mesh_axes, whole = ("y", "z_lo"), ("y", "z_lo", "z_hi", "x", "core")
    parts = lax.axis_size(mesh_axes)
    shape = jax.ShapeDtypeStruct
    packed, *picked = pl.pallas_call(
        select_kernel,
        out_shape=[shape((WIDTH, PACKED), jnp.bfloat16)]
        + [shape((WIDTH, GMAX * DOFS), jnp.bfloat16)] * NEIGH,
        in_specs=[SMEM, VMEM],
        out_specs=[VMEM] * (1 + NEIGH),
        compiler_params=pltpu.CompilerParams(vmem_limit_bytes=16 << 20),
        name="select",
    )(send_list, basis_vectors)
    arriving = []
    for block, offset in zip(picked, neighbour_offsets):
        route = [((i - offset) % parts, i) for i in range(parts)]
        arriving.append(lax.ppermute(block, mesh_axes, route))
    swap = [(0, 1), (1, 0)]
    blocks = pl.pallas_call(
        stage_kernel,
        out_shape=shape(stiffness_blocks.shape, jnp.bfloat16),
        in_specs=[VMEM],
        out_specs=VMEM,
        compiler_params=pltpu.CompilerParams(vmem_limit_bytes=24 << 20),
        cost_estimate=pl.CostEstimate(flops=0, bytes_accessed=12 << 20, transcendentals=0),
        name="stage",
    )(stiffness_blocks)
    line = lax.broadcasted_iota(jnp.int32, (8, CAP), 0)
    listed = jnp.where(line == 0, block_rows[None], block_columns[None])
    listed = jnp.where(line == 2, block_counts[0], listed).astype(jnp.float32)
    table = jnp.where(line == 3, density[None], listed)
    other_packed = lax.ppermute(packed, "x", [(i, i ^ NEAR) for i in range(4)])
    products = pl.pallas_call(
        block_kernel,
        out_shape=shape((WIDTH, PACKED), jnp.bfloat16),
        in_specs=[SMEM] + [VMEM] * (2 + NEIGH),
        out_specs=VMEM,
        scratch_shapes=[
            pltpu.VMEM((OWN + NEIGH * GMAX, WIDTH, DOFS), jnp.bfloat16),
            pltpu.VMEM((OWN, WIDTH, DOFS), jnp.float32),
        ],
        compiler_params=pltpu.CompilerParams(vmem_limit_bytes=24 << 20),
        name="blocks",
    )(table, packed, blocks, *arriving)
    other_packed, _ = lax.optimization_barrier((other_packed, products))
    pair = pl.pallas_call(
        join_kernel,
        out_shape=shape((2 * WIDTH, PACKED), jnp.bfloat16),
        in_specs=[VMEM] * 2,
        out_specs=VMEM,
        compiler_params=pltpu.CompilerParams(vmem_limit_bytes=8 << 20),
        name="join",
    )(packed, other_packed)
    over_z = lax.ppermute(products, "z_hi", swap)
    over_core = lax.ppermute(products, "core", swap)
    other_pair = lax.ppermute(pair, "x", [(i, i ^ FAR) for i in range(4)])
    place = jnp.stack([lax.axis_index(name) for name in ("z_hi", "x", "core")]).astype(jnp.int32)
    chunks_shape = shape((parts, 16, 128), jnp.bfloat16)
    begun = pl.pallas_call(
        own_tile_kernel,
        out_shape=chunks_shape,
        in_specs=[SMEM] + [VMEM] * 2,
        out_specs=VMEM,
        compiler_params=pltpu.CompilerParams(vmem_limit_bytes=16 << 20),
        cost_estimate=pl.CostEstimate(flops=2 << 23, bytes_accessed=1 << 20, transcendentals=0),
        name="own_tile",
    )(place, pair, products)
    behind, begun = lax.optimization_barrier((over_z, begun))
    over_both = lax.ppermute(behind, "core", swap)
    chunks = pl.pallas_call(
        tile_kernel,
        out_shape=chunks_shape,
        in_specs=[SMEM] + [VMEM] * 7,
        out_specs=VMEM,
        input_output_aliases={7: 0},
        compiler_params=pltpu.CompilerParams(vmem_limit_bytes=16 << 20),
        name="tile",
    )(place, pair, other_pair, products, over_core, over_z, over_both, begun)
    shares = lax.all_to_all(chunks, mesh_axes, 0, 0, tiled=True)
    block = pl.pallas_call(
        sum_kernel,
        out_shape=shape((32, WIDTH), jnp.float32),
        in_specs=[VMEM],
        out_specs=VMEM,
        compiler_params=pltpu.CompilerParams(vmem_limit_bytes=8 << 20),
        name="sum",
    )(shares)
    route = []
    for place in range(512):
        z2, a, c2, h, z, b, c = (int(i) for i in np.unravel_index(place, (2, 4, 2, 2, 2, 4, 2)))
        source = (z2 * 16 + a * 4 + c2 * 2 + h) * 16 + z * 8 + b * 2 + c
        target = (z2 * 16 + b * 4 + c2 * 2 + h) * 16 + z * 8 + a * 2 + c
        route.append((source, target))
    return lax.ppermute(block, whole, route).T


def solution(mesh):
    fine = Mesh(mesh.devices.reshape(8, 4, 2, 4, 2), ("y", "z_lo", "z_hi", "x", "core"))
    over_mesh, over_panel = ("y", "z_lo"), ("z_hi", "x", "core")
    placed = (
        P(over_mesh, over_panel, None),
        P(over_mesh, None, None),
        P(over_mesh),
        P(over_mesh),
        P(over_mesh),
        P(over_mesh),
        P(over_mesh),
    )
    return jax.shard_map(
        local, mesh=fine, in_specs=placed, out_specs=P(over_panel, over_mesh), check_vma=False
    )
```

```python
import jax
import jax.numpy as jnp
import numpy as np
from jax import lax
from jax.experimental import pallas as pl
from jax.experimental.pallas import tpu as pltpu
from jax.sharding import Mesh
from jax.sharding import PartitionSpec as P

GMAX = 4
NEIGH = 4
DOFS = 192
OWN = 8
WIDTH = 64
CAP = 56
PACKED = OWN * DOFS

neighbour_offsets = (1, -1, 2, -2)
ghost_order = (2, 3, 0, 1)
NEAR, FAR = 1, 3
VMEM = pl.BlockSpec(memory_space=pltpu.VMEM)
SMEM = pl.BlockSpec(memory_space=pltpu.SMEM)
HBM = pl.BlockSpec(memory_space=pltpu.HBM)


def pack_pair(first, second, out_ref, at):
    dtype = out_ref.dtype
    out_ref[:, at : at + 128] = first[:, :128].astype(dtype)
    out_ref[:, at + 128 : at + 256] = second[:, :128].astype(dtype)
    rest = jnp.concatenate([first[:, 128:], second[:, 128:]], axis=1)
    out_ref[:, at + 256 : at + 384] = rest.astype(dtype)


def select_kernel(send_ref, basis_ref, packed_ref, *ghost_refs):
    for neighbour, ghost_ref in enumerate(ghost_refs):
        for pair in range(GMAX // 2):
            at = neighbour * GMAX + 2 * pair
            pack_pair(
                basis_ref[send_ref[at]], basis_ref[send_ref[at + 1]], ghost_ref, 384 * pair
            )
    for pair in range(OWN // 2):
        pack_pair(basis_ref[2 * pair], basis_ref[2 * pair + 1], packed_ref, 384 * pair)


def stage_kernel(blocks_ref, blocks_out_ref):
    blocks_out_ref[...] = blocks_ref[...]


def join_kernel(own_ref, other_ref, pair_ref):
    pair_ref[:WIDTH] = own_ref[...]
    pair_ref[WIDTH:] = other_ref[...]


def block_kernel(table_ref, own_ref, blocks_ref, *rest):
    *ghost_refs, out_ref, pool, total = rest
    slots = [OWN + GMAX * neighbour for neighbour in ghost_order]
    for slot, slabs_ref in zip((0, *slots), (own_ref, *ghost_refs)):
        for at in range(0, slabs_ref.shape[1], 384):
            pool[slot, :, :128] = slabs_ref[:, at : at + 128]
            pool[slot + 1, :, :128] = slabs_ref[:, at + 128 : at + 256]
            pool[slot, :, 128:] = slabs_ref[:, at + 256 : at + 320]
            pool[slot + 1, :, 128:] = slabs_ref[:, at + 320 : at + 384]
            slot += 2
    total[...] = jnp.zeros_like(total)
    count = table_ref[2, 0].astype(jnp.int32)
    for block in range(CAP):
        row, column = table_ref[0, block].astype(jnp.int32), table_ref[1, block].astype(jnp.int32)
        product = lax.dot_general(
            pool[column],
            blocks_ref[block],
            (((1,), (1,)), ((), ())),
            preferred_element_type=jnp.float32,
        )
        density = table_ref[3, block]
        scale = jnp.where(block < count, 0.001 + density * density * density, 0.0)
        total[row] = total[row] + scale * product
    for pair in range(OWN // 2):
        pack_pair(total[2 * pair], total[2 * pair + 1], out_ref, 384 * pair)


def put_tile(place_ref, products, rows, out_ref, steps, row_step):
    low_lanes = lax.broadcasted_iota(jnp.int32, (16, 2 * WIDTH), 1) < WIDTH
    tile = lax.dot_general(
        products, rows, (((1,), (1,)), ((), ())), preferred_element_type=jnp.float32
    )
    x = place_ref[1] ^ row_step
    for index, (z_step, core_step) in enumerate(steps):
        half, core = place_ref[0] ^ z_step, place_ref[2] ^ core_step
        for h in range(2):
            at = WIDTH * index + 32 * h
            low, high = tile[at : at + 16], tile[at + 16 : at + 32]
            low_turned = pltpu.roll(low, WIDTH, 1)
            high_turned = pltpu.roll(high, WIDTH, 1)
            at = 16 * half + 2 * core + h
            first = jnp.where(low_lanes, low, high_turned)
            second = jnp.where(low_lanes, low_turned, high)
            out_ref[at + 4 * x] = first.astype(out_ref.dtype)
            out_ref[at + 4 * (x ^ NEAR)] = second.astype(out_ref.dtype)


def own_tile_kernel(place_ref, pair_ref, products_ref, out_ref):
    put_tile(place_ref, products_ref[...], pair_ref[...], out_ref, ((0, 0),), 0)


def most_tile_kernel(place_ref, pair_ref, other_pair_ref, *rest):
    *product_refs, begun_ref, out_ref = rest
    steps = ((0, 0), (0, 1), (1, 0))
    products = jnp.concatenate([ref[...] for ref in product_refs], axis=0)
    put_tile(place_ref, products, other_pair_ref[...], out_ref, steps, FAR)
    put_tile(place_ref, products[WIDTH:], pair_ref[...], out_ref, steps[1:], 0)


def last_tile_kernel(place_ref, pair_ref, other_pair_ref, products_ref, begun_ref, out_ref):
    products = products_ref[...]
    put_tile(place_ref, products, pair_ref[...], out_ref, ((1, 1),), 0)
    put_tile(place_ref, products, other_pair_ref[...], out_ref, ((1, 1),), FAR)


def sum_kernel(parts_ref, out_ref):
    total = jnp.sum(parts_ref[...].astype(jnp.float32), axis=0)
    out_ref[:16] = total[:, :WIDTH]
    out_ref[16:] = total[:, WIDTH:]


def local(
    basis_vectors, stiffness_blocks, block_rows, block_columns, density, block_counts, send_list
):
    mesh_axes, whole = ("y", "z_lo"), ("y", "z_lo", "z_hi", "x", "core")
    parts = lax.axis_size(mesh_axes)
    shape = jax.ShapeDtypeStruct
    packed, *picked = pl.pallas_call(
        select_kernel,
        out_shape=[shape((WIDTH, PACKED), jnp.bfloat16)]
        + [shape((WIDTH, GMAX * DOFS), jnp.bfloat16)] * NEIGH,
        in_specs=[SMEM, VMEM],
        out_specs=[VMEM] * (1 + NEIGH),
        compiler_params=pltpu.CompilerParams(vmem_limit_bytes=16 << 20),
        name="select",
    )(send_list, basis_vectors)
    arriving = [None] * NEIGH
    for neighbour in ghost_order:
        offset = neighbour_offsets[neighbour]
        route = [((i - offset) % parts, i) for i in range(parts)]
        arriving[neighbour] = lax.ppermute(picked[neighbour], mesh_axes, route)
    swap = [(0, 1), (1, 0)]
    blocks = pl.pallas_call(
        stage_kernel,
        out_shape=shape(stiffness_blocks.shape, jnp.bfloat16),
        in_specs=[VMEM],
        out_specs=VMEM,
        compiler_params=pltpu.CompilerParams(vmem_limit_bytes=24 << 20),
        cost_estimate=pl.CostEstimate(flops=0, bytes_accessed=12 << 20, transcendentals=0),
        name="stage",
    )(stiffness_blocks)
    line = lax.broadcasted_iota(jnp.int32, (8, CAP), 0)
    listed = jnp.where(line == 0, block_rows[None], block_columns[None])
    listed = jnp.where(line == 2, block_counts[0], listed).astype(jnp.float32)
    table = jnp.where(line == 3, density[None], listed)
    other_packed = lax.ppermute(packed, "x", [(i, i ^ NEAR) for i in range(4)])
    products = pl.pallas_call(
        block_kernel,
        out_shape=shape((WIDTH, PACKED), jnp.bfloat16),
        in_specs=[SMEM] + [VMEM] * (2 + NEIGH),
        out_specs=VMEM,
        scratch_shapes=[
            pltpu.VMEM((OWN + NEIGH * GMAX, WIDTH, DOFS), jnp.bfloat16),
            pltpu.VMEM((OWN, WIDTH, DOFS), jnp.float32),
        ],
        compiler_params=pltpu.CompilerParams(vmem_limit_bytes=24 << 20),
        name="blocks",
    )(table, packed, blocks, *(arriving[neighbour] for neighbour in ghost_order))
    other_packed, _ = lax.optimization_barrier((other_packed, products))
    pair = pl.pallas_call(
        join_kernel,
        out_shape=shape((2 * WIDTH, PACKED), jnp.bfloat16),
        in_specs=[VMEM] * 2,
        out_specs=VMEM,
        compiler_params=pltpu.CompilerParams(vmem_limit_bytes=8 << 20),
        name="join",
    )(packed, other_packed)
    over_z = lax.ppermute(products, "z_hi", swap)
    over_core = lax.ppermute(products, "core", swap)
    other_pair = lax.ppermute(pair, "x", [(i, i ^ FAR) for i in range(4)])
    place = jnp.stack([lax.axis_index(name) for name in ("z_hi", "x", "core")]).astype(jnp.int32)
    chunks_shape = shape((parts, 16, 128), jnp.bfloat16)
    begun = pl.pallas_call(
        own_tile_kernel,
        out_shape=chunks_shape,
        in_specs=[SMEM] + [VMEM] * 2,
        out_specs=VMEM,
        compiler_params=pltpu.CompilerParams(vmem_limit_bytes=16 << 20),
        cost_estimate=pl.CostEstimate(flops=2 << 23, bytes_accessed=1 << 20, transcendentals=0),
        name="own_tile",
    )(place, pair, products)
    behind, begun = lax.optimization_barrier((over_z, begun))
    over_both = lax.ppermute(behind, "core", swap)
    begun = pl.pallas_call(
        most_tile_kernel,
        out_shape=chunks_shape,
        in_specs=[SMEM] + [VMEM] * 6,
        out_specs=VMEM,
        input_output_aliases={6: 0},
        compiler_params=pltpu.CompilerParams(vmem_limit_bytes=16 << 20),
        name="most_tile",
    )(place, pair, other_pair, products, over_core, over_z, begun)
    chunks = pl.pallas_call(
        last_tile_kernel,
        out_shape=chunks_shape,
        in_specs=[SMEM] + [VMEM] * 4,
        out_specs=VMEM,
        input_output_aliases={4: 0},
        compiler_params=pltpu.CompilerParams(vmem_limit_bytes=16 << 20),
        name="tile",
    )(place, pair, other_pair, over_both, begun)
    shares = lax.all_to_all(chunks, mesh_axes, 0, 0, tiled=True)
    block = pl.pallas_call(
        sum_kernel,
        out_shape=shape((32, WIDTH), jnp.float32),
        in_specs=[VMEM],
        out_specs=VMEM,
        compiler_params=pltpu.CompilerParams(vmem_limit_bytes=8 << 20),
        name="sum",
    )(shares)
    route = []
    for place in range(512):
        z2, a, c2, h, z, b, c = (int(i) for i in np.unravel_index(place, (2, 4, 2, 2, 2, 4, 2)))
        source = (z2 * 16 + a * 4 + c2 * 2 + h) * 16 + z * 8 + b * 2 + c
        target = (z2 * 16 + b * 4 + c2 * 2 + h) * 16 + z * 8 + a * 2 + c
        route.append((source, target))
    return lax.ppermute(block, whole, route).T


def solution(mesh):
    fine = Mesh(mesh.devices.reshape(8, 4, 2, 4, 2), ("y", "z_lo", "z_hi", "x", "core"))
    over_mesh, over_panel = ("y", "z_lo"), ("z_hi", "x", "core")
    placed = (
        P(over_mesh, over_panel, None),
        P(over_mesh, None, None),
        P(over_mesh),
        P(over_mesh),
        P(over_mesh),
        P(over_mesh),
        P(over_mesh),
    )
    return jax.shard_map(
        local, mesh=fine, in_specs=placed, out_specs=P(over_panel, over_mesh), check_vma=False
    )
```

```python
import jax
import jax.numpy as jnp
import numpy as np
from jax import lax
from jax.experimental import pallas as pl
from jax.experimental.pallas import tpu as pltpu
from jax.sharding import Mesh
from jax.sharding import PartitionSpec as P

GMAX = 4
NEIGH = 4
DOFS = 192
OWN = 8
WIDTH = 64
CAP = 56
PACKED = OWN * DOFS

neighbour_offsets = (1, -1, 2, -2)
ghost_order = (2, 3, 0, 1)
NEAR, FAR = 1, 3
VMEM = pl.BlockSpec(memory_space=pltpu.VMEM)
SMEM = pl.BlockSpec(memory_space=pltpu.SMEM)
HBM = pl.BlockSpec(memory_space=pltpu.HBM)


def pack_pair(first, second, out_ref, at):
    dtype = out_ref.dtype
    out_ref[:, at : at + 128] = first[:, :128].astype(dtype)
    out_ref[:, at + 128 : at + 256] = second[:, :128].astype(dtype)
    rest = jnp.concatenate([first[:, 128:], second[:, 128:]], axis=1)
    out_ref[:, at + 256 : at + 384] = rest.astype(dtype)


def select_kernel(send_ref, basis_ref, packed_ref, *ghost_refs):
    for neighbour, ghost_ref in enumerate(ghost_refs):
        for pair in range(GMAX // 2):
            at = neighbour * GMAX + 2 * pair
            pack_pair(
                basis_ref[send_ref[at]], basis_ref[send_ref[at + 1]], ghost_ref, 384 * pair
            )
    for pair in range(OWN // 2):
        pack_pair(basis_ref[2 * pair], basis_ref[2 * pair + 1], packed_ref, 384 * pair)


def stage_kernel(blocks_ref, blocks_out_ref):
    blocks_out_ref[...] = blocks_ref[...]


def join_kernel(own_ref, other_ref, pair_ref):
    pair_ref[:WIDTH] = own_ref[...]
    pair_ref[WIDTH:] = other_ref[...]


def block_kernel(table_ref, own_ref, blocks_ref, *rest):
    *ghost_refs, out_ref, pool, total = rest
    slots = [OWN + GMAX * neighbour for neighbour in ghost_order]
    for slot, slabs_ref in zip((0, *slots), (own_ref, *ghost_refs)):
        for at in range(0, slabs_ref.shape[1], 384):
            pool[slot, :, :128] = slabs_ref[:, at : at + 128]
            pool[slot + 1, :, :128] = slabs_ref[:, at + 128 : at + 256]
            pool[slot, :, 128:] = slabs_ref[:, at + 256 : at + 320]
            pool[slot + 1, :, 128:] = slabs_ref[:, at + 320 : at + 384]
            slot += 2
    total[...] = jnp.zeros_like(total)
    count = table_ref[2, 0].astype(jnp.int32)
    for block in range(CAP):
        row, column = table_ref[0, block].astype(jnp.int32), table_ref[1, block].astype(jnp.int32)
        product = lax.dot_general(
            pool[column],
            blocks_ref[block],
            (((1,), (1,)), ((), ())),
            preferred_element_type=jnp.float32,
        )
        density = table_ref[3, block]
        scale = jnp.where(block < count, 0.001 + density * density * density, 0.0)
        total[row] = total[row] + scale * product
    for pair in range(OWN // 2):
        pack_pair(total[2 * pair], total[2 * pair + 1], out_ref, 384 * pair)


def put_tile(place_ref, products, rows, out_ref, steps, row_step):
    low_lanes = lax.broadcasted_iota(jnp.int32, (16, 2 * WIDTH), 1) < WIDTH
    tile = lax.dot_general(
        products, rows, (((1,), (1,)), ((), ())), preferred_element_type=jnp.float32
    )
    x = place_ref[1] ^ row_step
    for index, (z_step, core_step) in enumerate(steps):
        half, core = place_ref[0] ^ z_step, place_ref[2] ^ core_step
        for h in range(2):
            at = WIDTH * index + 32 * h
            low, high = tile[at : at + 16], tile[at + 16 : at + 32]
            low_turned = pltpu.roll(low, WIDTH, 1)
            high_turned = pltpu.roll(high, WIDTH, 1)
            at = 16 * half + 2 * core + h
            first = jnp.where(low_lanes, low, high_turned)
            second = jnp.where(low_lanes, low_turned, high)
            out_ref[at + 4 * x] = first.astype(out_ref.dtype)
            out_ref[at + 4 * (x ^ NEAR)] = second.astype(out_ref.dtype)


def own_tile_kernel(place_ref, pair_ref, products_ref, out_ref):
    put_tile(place_ref, products_ref[...], pair_ref[...], out_ref, ((0, 0),), 0)


def tile_kernel(place_ref, pair_ref, other_pair_ref, *rest):
    *product_refs, begun_ref, out_ref = rest
    steps = ((0, 0), (0, 1), (1, 0), (1, 1))
    products = jnp.concatenate([ref[...] for ref in product_refs], axis=0)
    put_tile(place_ref, products, other_pair_ref[...], out_ref, steps, FAR)
    put_tile(place_ref, products[WIDTH:], pair_ref[...], out_ref, steps[1:], 0)


def sum_kernel(parts_ref, out_ref):
    total = jnp.sum(parts_ref[...].astype(jnp.float32), axis=0)
    out_ref[:16] = total[:, :WIDTH]
    out_ref[16:] = total[:, WIDTH:]


def local(
    basis_vectors, stiffness_blocks, block_rows, block_columns, density, block_counts, send_list
):
    mesh_axes, whole = ("y", "z_lo"), ("y", "z_lo", "z_hi", "x", "core")
    parts = lax.axis_size(mesh_axes)
    shape = jax.ShapeDtypeStruct
    packed, *picked = pl.pallas_call(
        select_kernel,
        out_shape=[shape((WIDTH, PACKED), jnp.bfloat16)]
        + [shape((WIDTH, GMAX * DOFS), jnp.bfloat16)] * NEIGH,
        in_specs=[SMEM, VMEM],
        out_specs=[VMEM] * (1 + NEIGH),
        compiler_params=pltpu.CompilerParams(vmem_limit_bytes=16 << 20),
        name="select",
    )(send_list, basis_vectors)
    arriving = []
    for neighbour in ghost_order:
        offset = neighbour_offsets[neighbour]
        route = [((i - offset) % parts, i) for i in range(parts)]
        arriving.append(lax.ppermute(picked[neighbour], mesh_axes, route))
    swap = [(0, 1), (1, 0)]
    blocks = pl.pallas_call(
        stage_kernel,
        out_shape=shape(stiffness_blocks.shape, jnp.bfloat16),
        in_specs=[VMEM],
        out_specs=VMEM,
        compiler_params=pltpu.CompilerParams(vmem_limit_bytes=24 << 20),
        cost_estimate=pl.CostEstimate(flops=0, bytes_accessed=12 << 20, transcendentals=0),
        name="stage",
    )(stiffness_blocks)
    line = lax.broadcasted_iota(jnp.int32, (8, CAP), 0)
    listed = jnp.where(line == 0, block_rows[None], block_columns[None])
    listed = jnp.where(line == 2, block_counts[0], listed).astype(jnp.float32)
    table = jnp.where(line == 3, density[None], listed)
    other_packed = lax.ppermute(packed, "x", [(i, i ^ NEAR) for i in range(4)])
    products = pl.pallas_call(
        block_kernel,
        out_shape=shape((WIDTH, PACKED), jnp.bfloat16),
        in_specs=[SMEM] + [VMEM] * (2 + NEIGH),
        out_specs=VMEM,
        scratch_shapes=[
            pltpu.VMEM((OWN + NEIGH * GMAX, WIDTH, DOFS), jnp.bfloat16),
            pltpu.VMEM((OWN, WIDTH, DOFS), jnp.float32),
        ],
        compiler_params=pltpu.CompilerParams(vmem_limit_bytes=24 << 20),
        name="blocks",
    )(table, packed, blocks, *arriving)
    other_packed, _ = lax.optimization_barrier((other_packed, products))
    pair = pl.pallas_call(
        join_kernel,
        out_shape=shape((2 * WIDTH, PACKED), jnp.bfloat16),
        in_specs=[VMEM] * 2,
        out_specs=VMEM,
        compiler_params=pltpu.CompilerParams(vmem_limit_bytes=8 << 20),
        name="join",
    )(packed, other_packed)
    over_z = lax.ppermute(products, "z_hi", swap)
    over_core = lax.ppermute(products, "core", swap)
    other_pair = lax.ppermute(pair, "x", [(i, i ^ FAR) for i in range(4)])
    place = jnp.stack([lax.axis_index(name) for name in ("z_hi", "x", "core")]).astype(jnp.int32)
    chunks_shape = shape((parts, 16, 128), jnp.bfloat16)
    begun = pl.pallas_call(
        own_tile_kernel,
        out_shape=chunks_shape,
        in_specs=[SMEM] + [VMEM] * 2,
        out_specs=VMEM,
        compiler_params=pltpu.CompilerParams(vmem_limit_bytes=16 << 20),
        cost_estimate=pl.CostEstimate(flops=2 << 23, bytes_accessed=1 << 20, transcendentals=0),
        name="own_tile",
    )(place, pair, products)
    behind, begun = lax.optimization_barrier((over_z, begun))
    over_both = lax.ppermute(behind, "core", swap)
    chunks = pl.pallas_call(
        tile_kernel,
        out_shape=chunks_shape,
        in_specs=[SMEM] + [VMEM] * 7,
        out_specs=VMEM,
        input_output_aliases={7: 0},
        compiler_params=pltpu.CompilerParams(vmem_limit_bytes=16 << 20),
        name="tile",
    )(place, pair, other_pair, products, over_core, over_z, over_both, begun)
    shares = lax.all_to_all(chunks, mesh_axes, 0, 0, tiled=True)
    block = pl.pallas_call(
        sum_kernel,
        out_shape=shape((32, WIDTH), jnp.float32),
        in_specs=[VMEM],
        out_specs=VMEM,
        compiler_params=pltpu.CompilerParams(vmem_limit_bytes=8 << 20),
        name="sum",
    )(shares)
    route = []
    for place in range(512):
        z2, a, c2, h, z, b, c = (int(i) for i in np.unravel_index(place, (2, 4, 2, 2, 2, 4, 2)))
        source = (z2 * 16 + a * 4 + c2 * 2 + h) * 16 + z * 8 + b * 2 + c
        target = (z2 * 16 + b * 4 + c2 * 2 + h) * 16 + z * 8 + a * 2 + c
        route.append((source, target))
    return lax.ppermute(block, whole, route).T


def solution(mesh):
    fine = Mesh(mesh.devices.reshape(8, 4, 2, 4, 2), ("y", "z_lo", "z_hi", "x", "core"))
    over_mesh, over_panel = ("y", "z_lo"), ("z_hi", "x", "core")
    placed = (
        P(over_mesh, over_panel, None),
        P(over_mesh, None, None),
        P(over_mesh),
        P(over_mesh),
        P(over_mesh),
        P(over_mesh),
        P(over_mesh),
    )
    return jax.shard_map(
        local, mesh=fine, in_specs=placed, out_specs=P(over_panel, over_mesh), check_vma=False
    )
```

```python
import jax
import jax.numpy as jnp
import numpy as np
from jax import lax
from jax.experimental import pallas as pl
from jax.experimental.pallas import tpu as pltpu
from jax.sharding import Mesh
from jax.sharding import PartitionSpec as P

GMAX = 4
NEIGH = 4
DOFS = 192
OWN = 8
WIDTH = 64
CAP = 56
PACKED = OWN * DOFS

neighbour_offsets = (1, -1, 2, -2)
NEAR, FAR = 1, 3
VMEM = pl.BlockSpec(memory_space=pltpu.VMEM)
SMEM = pl.BlockSpec(memory_space=pltpu.SMEM)
HBM = pl.BlockSpec(memory_space=pltpu.HBM)


def pack_pair(first, second, out_ref, at):
    dtype = out_ref.dtype
    out_ref[:, at : at + 128] = first[:, :128].astype(dtype)
    out_ref[:, at + 128 : at + 256] = second[:, :128].astype(dtype)
    rest = jnp.concatenate([first[:, 128:], second[:, 128:]], axis=1)
    out_ref[:, at + 256 : at + 384] = rest.astype(dtype)


def select_kernel(send_ref, basis_ref, packed_ref, *ghost_refs):
    for neighbour, ghost_ref in enumerate(ghost_refs):
        for pair in range(GMAX // 2):
            at = neighbour * GMAX + 2 * pair
            pack_pair(
                basis_ref[send_ref[at]], basis_ref[send_ref[at + 1]], ghost_ref, 384 * pair
            )
    for pair in range(OWN // 2):
        pack_pair(basis_ref[2 * pair], basis_ref[2 * pair + 1], packed_ref, 384 * pair)


def stage_kernel(blocks_ref, blocks_out_ref):
    blocks_out_ref[...] = blocks_ref[...]


def join_kernel(own_ref, other_ref, pair_ref):
    pair_ref[:WIDTH] = own_ref[...]
    pair_ref[WIDTH:] = other_ref[...]


def block_kernel(table_ref, own_ref, blocks_ref, *rest):
    *ghost_refs, out_ref, pool, total = rest
    slot = 0
    for slabs_ref in (own_ref, *ghost_refs):
        for at in range(0, slabs_ref.shape[1], 384):
            pool[slot, :, :128] = slabs_ref[:, at : at + 128]
            pool[slot + 1, :, :128] = slabs_ref[:, at + 128 : at + 256]
            pool[slot, :, 128:] = slabs_ref[:, at + 256 : at + 320]
            pool[slot + 1, :, 128:] = slabs_ref[:, at + 320 : at + 384]
            slot += 2
    total[...] = jnp.zeros_like(total)
    count = table_ref[2, 0].astype(jnp.int32)
    for block in range(CAP):
        row, column = table_ref[0, block].astype(jnp.int32), table_ref[1, block].astype(jnp.int32)
        product = lax.dot_general(
            pool[column],
            blocks_ref[block],
            (((1,), (1,)), ((), ())),
            preferred_element_type=jnp.float32,
        )
        density = table_ref[3, block]
        scale = jnp.where(block < count, 0.001 + density * density * density, 0.0)
        total[row] = total[row] + scale * product
    for pair in range(OWN // 2):
        pack_pair(total[2 * pair], total[2 * pair + 1], out_ref, 384 * pair)


def put_tile(place_ref, products, rows, out_ref, steps, row_step):
    low_lanes = lax.broadcasted_iota(jnp.int32, (16, 2 * WIDTH), 1) < WIDTH
    tile = lax.dot_general(
        products, rows, (((1,), (1,)), ((), ())), preferred_element_type=jnp.float32
    )
    x = place_ref[1] ^ row_step
    for index, (z_step, core_step) in enumerate(steps):
        half, core = place_ref[0] ^ z_step, place_ref[2] ^ core_step
        for h in range(2):
            at = WIDTH * index + 32 * h
            low, high = tile[at : at + 16], tile[at + 16 : at + 32]
            low_turned = pltpu.roll(low, WIDTH, 1)
            high_turned = pltpu.roll(high, WIDTH, 1)
            at = 16 * half + 2 * core + h
            first = jnp.where(low_lanes, low, high_turned)
            second = jnp.where(low_lanes, low_turned, high)
            out_ref[at + 4 * x] = first.astype(out_ref.dtype)
            out_ref[at + 4 * (x ^ NEAR)] = second.astype(out_ref.dtype)


def own_tile_kernel(place_ref, pair_ref, products_ref, out_ref):
    put_tile(place_ref, products_ref[...], pair_ref[...], out_ref, ((0, 0),), 0)


def tile_kernel(place_ref, pair_ref, other_pair_ref, *rest):
    *product_refs, begun_ref, out_ref = rest
    steps = ((0, 0), (0, 1), (1, 0), (1, 1))
    products = jnp.concatenate([ref[...] for ref in product_refs], axis=0)
    put_tile(place_ref, products, other_pair_ref[...], out_ref, steps, FAR)
    put_tile(place_ref, products[WIDTH:], pair_ref[...], out_ref, steps[1:], 0)


def sum_kernel(parts_ref, out_ref):
    total = jnp.sum(parts_ref[...].astype(jnp.float32), axis=0)
    out_ref[:16] = total[:, :WIDTH]
    out_ref[16:] = total[:, WIDTH:]


def local(
    basis_vectors, stiffness_blocks, block_rows, block_columns, density, block_counts, send_list
):
    mesh_axes, whole = ("y", "z_lo"), ("y", "z_lo", "z_hi", "x", "core")
    parts = lax.axis_size(mesh_axes)
    shape = jax.ShapeDtypeStruct
    packed, *picked = pl.pallas_call(
        select_kernel,
        out_shape=[shape((WIDTH, PACKED), jnp.bfloat16)]
        + [shape((WIDTH, GMAX * DOFS), jnp.bfloat16)] * NEIGH,
        in_specs=[SMEM, VMEM],
        out_specs=[VMEM] * (1 + NEIGH),
        compiler_params=pltpu.CompilerParams(vmem_limit_bytes=16 << 20),
        name="select",
    )(send_list, basis_vectors)
    arriving = []
    for block, offset in zip(picked, neighbour_offsets):
        route = [((i - offset) % parts, i) for i in range(parts)]
        arriving.append(lax.ppermute(block, mesh_axes, route))
    swap = [(0, 1), (1, 0)]
    blocks = pl.pallas_call(
        stage_kernel,
        out_shape=shape(stiffness_blocks.shape, jnp.bfloat16),
        in_specs=[VMEM],
        out_specs=VMEM,
        compiler_params=pltpu.CompilerParams(vmem_limit_bytes=24 << 20),
        cost_estimate=pl.CostEstimate(flops=0, bytes_accessed=12 << 20, transcendentals=0),
        name="stage",
    )(stiffness_blocks)
    line = lax.broadcasted_iota(jnp.int32, (8, CAP), 0)
    listed = jnp.where(line == 0, block_rows[None], block_columns[None])
    listed = jnp.where(line == 2, block_counts[0], listed).astype(jnp.float32)
    table = jnp.where(line == 3, density[None], listed)
    other_packed = lax.ppermute(packed, "x", [(i, i ^ NEAR) for i in range(4)])
    products = pl.pallas_call(
        block_kernel,
        out_shape=shape((WIDTH, PACKED), jnp.bfloat16),
        in_specs=[SMEM] + [VMEM] * (2 + NEIGH),
        out_specs=VMEM,
        scratch_shapes=[
            pltpu.VMEM((OWN + NEIGH * GMAX, WIDTH, DOFS), jnp.bfloat16),
            pltpu.VMEM((OWN, WIDTH, DOFS), jnp.float32),
        ],
        compiler_params=pltpu.CompilerParams(vmem_limit_bytes=24 << 20),
        name="blocks",
    )(table, packed, blocks, *arriving)
    other_packed, _ = lax.optimization_barrier((other_packed, products))
    pair = pl.pallas_call(
        join_kernel,
        out_shape=shape((2 * WIDTH, PACKED), jnp.bfloat16),
        in_specs=[VMEM] * 2,
        out_specs=VMEM,
        compiler_params=pltpu.CompilerParams(vmem_limit_bytes=8 << 20),
        name="join",
    )(packed, other_packed)
    over_z = lax.ppermute(products, "z_hi", swap)
    over_core = lax.ppermute(products, "core", swap)
    other_pair = lax.ppermute(pair, "x", [(i, i ^ FAR) for i in range(4)])
    place = jnp.stack([lax.axis_index(name) for name in ("z_hi", "x", "core")]).astype(jnp.int32)
    chunks_shape = shape((parts, 16, 128), jnp.bfloat16)
    over_both = lax.ppermute(over_z, "core", swap)
    behind, over_z = lax.optimization_barrier((products, over_z))
    begun = pl.pallas_call(
        own_tile_kernel,
        out_shape=chunks_shape,
        in_specs=[SMEM] + [VMEM] * 2,
        out_specs=VMEM,
        compiler_params=pltpu.CompilerParams(vmem_limit_bytes=16 << 20),
        cost_estimate=pl.CostEstimate(flops=2 << 23, bytes_accessed=1 << 20, transcendentals=0),
        name="own_tile",
    )(place, pair, behind)
    chunks = pl.pallas_call(
        tile_kernel,
        out_shape=chunks_shape,
        in_specs=[SMEM] + [VMEM] * 7,
        out_specs=VMEM,
        input_output_aliases={7: 0},
        compiler_params=pltpu.CompilerParams(vmem_limit_bytes=16 << 20),
        name="tile",
    )(place, pair, other_pair, products, over_core, over_z, over_both, begun)
    shares = lax.all_to_all(chunks, mesh_axes, 0, 0, tiled=True)
    block = pl.pallas_call(
        sum_kernel,
        out_shape=shape((32, WIDTH), jnp.float32),
        in_specs=[VMEM],
        out_specs=VMEM,
        compiler_params=pltpu.CompilerParams(vmem_limit_bytes=8 << 20),
        name="sum",
    )(shares)
    route = []
    for place in range(512):
        z2, a, c2, h, z, b, c = (int(i) for i in np.unravel_index(place, (2, 4, 2, 2, 2, 4, 2)))
        source = (z2 * 16 + a * 4 + c2 * 2 + h) * 16 + z * 8 + b * 2 + c
        target = (z2 * 16 + b * 4 + c2 * 2 + h) * 16 + z * 8 + a * 2 + c
        route.append((source, target))
    return lax.ppermute(block, whole, route).T


def solution(mesh):
    fine = Mesh(mesh.devices.reshape(8, 4, 2, 4, 2), ("y", "z_lo", "z_hi", "x", "core"))
    over_mesh, over_panel = ("y", "z_lo"), ("z_hi", "x", "core")
    placed = (
        P(over_mesh, over_panel, None),
        P(over_mesh, None, None),
        P(over_mesh),
        P(over_mesh),
        P(over_mesh),
        P(over_mesh),
        P(over_mesh),
    )
    return jax.shard_map(
        local, mesh=fine, in_specs=placed, out_specs=P(over_panel, over_mesh), check_vma=False
    )
```

```python
import jax
import jax.numpy as jnp
import numpy as np
from jax import lax
from jax.experimental import pallas as pl
from jax.experimental.pallas import tpu as pltpu
from jax.sharding import Mesh
from jax.sharding import PartitionSpec as P

GMAX = 4
NEIGH = 4
DOFS = 192
OWN = 8
WIDTH = 64
CAP = 56
PACKED = OWN * DOFS

neighbour_offsets = (1, -1, 2, -2)
ghost_order = (2, 3, 0, 1)
NEAR, FAR = 1, 3
VMEM = pl.BlockSpec(memory_space=pltpu.VMEM)
SMEM = pl.BlockSpec(memory_space=pltpu.SMEM)
HBM = pl.BlockSpec(memory_space=pltpu.HBM)


def pack_pair(first, second, out_ref, at):
    dtype = out_ref.dtype
    out_ref[:, at : at + 128] = first[:, :128].astype(dtype)
    out_ref[:, at + 128 : at + 256] = second[:, :128].astype(dtype)
    rest = jnp.concatenate([first[:, 128:], second[:, 128:]], axis=1)
    out_ref[:, at + 256 : at + 384] = rest.astype(dtype)


def select_kernel(send_ref, basis_ref, packed_ref, *ghost_refs):
    for neighbour, ghost_ref in enumerate(ghost_refs):
        for pair in range(GMAX // 2):
            at = neighbour * GMAX + 2 * pair
            pack_pair(
                basis_ref[send_ref[at]], basis_ref[send_ref[at + 1]], ghost_ref, 384 * pair
            )
    for pair in range(OWN // 2):
        pack_pair(basis_ref[2 * pair], basis_ref[2 * pair + 1], packed_ref, 384 * pair)


def stage_kernel(blocks_ref, blocks_out_ref):
    blocks_out_ref[...] = blocks_ref[...]


def join_kernel(own_ref, other_ref, pair_ref):
    pair_ref[:WIDTH] = own_ref[...]
    pair_ref[WIDTH:] = other_ref[...]


def block_kernel(table_ref, own_ref, blocks_ref, *rest):
    *ghost_refs, out_ref, pool, total = rest
    slots = [OWN + GMAX * neighbour for neighbour in ghost_order]
    for slot, slabs_ref in zip((0, *slots), (own_ref, *ghost_refs)):
        for at in range(0, slabs_ref.shape[1], 384):
            pool[slot, :, :128] = slabs_ref[:, at : at + 128]
            pool[slot + 1, :, :128] = slabs_ref[:, at + 128 : at + 256]
            pool[slot, :, 128:] = slabs_ref[:, at + 256 : at + 320]
            pool[slot + 1, :, 128:] = slabs_ref[:, at + 320 : at + 384]
            slot += 2
    total[...] = jnp.zeros_like(total)
    count = table_ref[2, 0].astype(jnp.int32)
    for block in range(CAP):
        row, column = table_ref[0, block].astype(jnp.int32), table_ref[1, block].astype(jnp.int32)
        product = lax.dot_general(
            pool[column],
            blocks_ref[block],
            (((1,), (1,)), ((), ())),
            preferred_element_type=jnp.float32,
        )
        density = table_ref[3, block]
        scale = jnp.where(block < count, 0.001 + density * density * density, 0.0)
        total[row] = total[row] + scale * product
    for pair in range(OWN // 2):
        pack_pair(total[2 * pair], total[2 * pair + 1], out_ref, 384 * pair)


def put_tile(place_ref, products, rows, out_ref, steps, row_step):
    low_lanes = lax.broadcasted_iota(jnp.int32, (16, 2 * WIDTH), 1) < WIDTH
    tile = lax.dot_general(
        products, rows, (((1,), (1,)), ((), ())), preferred_element_type=jnp.float32
    )
    x = place_ref[1] ^ row_step
    for index, (z_step, core_step) in enumerate(steps):
        half, core = place_ref[0] ^ z_step, place_ref[2] ^ core_step
        for h in range(2):
            at = WIDTH * index + 32 * h
            low, high = tile[at : at + 16], tile[at + 16 : at + 32]
            low_turned = pltpu.roll(low, WIDTH, 1)
            high_turned = pltpu.roll(high, WIDTH, 1)
            at = 16 * half + 2 * core + h
            first = jnp.where(low_lanes, low, high_turned)
            second = jnp.where(low_lanes, low_turned, high)
            out_ref[at + 4 * x] = first.astype(out_ref.dtype)
            out_ref[at + 4 * (x ^ NEAR)] = second.astype(out_ref.dtype)


def own_tile_kernel(place_ref, pair_ref, products_ref, out_ref):
    put_tile(place_ref, products_ref[...], pair_ref[...], out_ref, ((0, 0),), 0)


def tile_kernel(place_ref, pair_ref, other_pair_ref, *rest):
    *product_refs, begun_ref, out_ref = rest
    steps = ((0, 0), (0, 1), (1, 0), (1, 1))
    products = jnp.concatenate([ref[...] for ref in product_refs], axis=0)
    put_tile(place_ref, products, other_pair_ref[...], out_ref, steps, FAR)
    put_tile(place_ref, products[WIDTH:], pair_ref[...], out_ref, steps[1:], 0)


def sum_kernel(parts_ref, out_ref):
    total = jnp.sum(parts_ref[...].astype(jnp.float32), axis=0)
    out_ref[:16] = total[:, :WIDTH]
    out_ref[16:] = total[:, WIDTH:]


def local(
    basis_vectors, stiffness_blocks, block_rows, block_columns, density, block_counts, send_list
):
    mesh_axes, whole = ("y", "z_lo"), ("y", "z_lo", "z_hi", "x", "core")
    parts = lax.axis_size(mesh_axes)
    shape = jax.ShapeDtypeStruct
    packed, *picked = pl.pallas_call(
        select_kernel,
        out_shape=[shape((WIDTH, PACKED), jnp.bfloat16)]
        + [shape((WIDTH, GMAX * DOFS), jnp.bfloat16)] * NEIGH,
        in_specs=[SMEM, VMEM],
        out_specs=[VMEM] * (1 + NEIGH),
        compiler_params=pltpu.CompilerParams(vmem_limit_bytes=16 << 20),
        name="select",
    )(send_list, basis_vectors)
    arriving = []
    for neighbour in ghost_order:
        offset = neighbour_offsets[neighbour]
        route = [((i - offset) % parts, i) for i in range(parts)]
        arriving.append(lax.ppermute(picked[neighbour], mesh_axes, route))
    swap = [(0, 1), (1, 0)]
    blocks = pl.pallas_call(
        stage_kernel,
        out_shape=shape(stiffness_blocks.shape, jnp.bfloat16),
        in_specs=[VMEM],
        out_specs=VMEM,
        compiler_params=pltpu.CompilerParams(vmem_limit_bytes=24 << 20),
        cost_estimate=pl.CostEstimate(flops=0, bytes_accessed=12 << 20, transcendentals=0),
        name="stage",
    )(stiffness_blocks)
    line = lax.broadcasted_iota(jnp.int32, (8, CAP), 0)
    listed = jnp.where(line == 0, block_rows[None], block_columns[None])
    listed = jnp.where(line == 2, block_counts[0], listed).astype(jnp.float32)
    table = jnp.where(line == 3, density[None], listed)
    other_packed = lax.ppermute(packed, "x", [(i, i ^ NEAR) for i in range(4)])
    products = pl.pallas_call(
        block_kernel,
        out_shape=shape((WIDTH, PACKED), jnp.bfloat16),
        in_specs=[SMEM] + [VMEM] * (2 + NEIGH),
        out_specs=VMEM,
        scratch_shapes=[
            pltpu.VMEM((OWN + NEIGH * GMAX, WIDTH, DOFS), jnp.bfloat16),
            pltpu.VMEM((OWN, WIDTH, DOFS), jnp.float32),
        ],
        compiler_params=pltpu.CompilerParams(vmem_limit_bytes=24 << 20),
        name="blocks",
    )(table, packed, blocks, *arriving)
    other_packed, _ = lax.optimization_barrier((other_packed, products))
    pair = pl.pallas_call(
        join_kernel,
        out_shape=shape((2 * WIDTH, PACKED), jnp.bfloat16),
        in_specs=[VMEM] * 2,
        out_specs=VMEM,
        compiler_params=pltpu.CompilerParams(vmem_limit_bytes=8 << 20),
        name="join",
    )(packed, other_packed)
    over_z = lax.ppermute(products, "z_hi", swap)
    over_core = lax.ppermute(products, "core", swap)
    other_pair = lax.ppermute(pair, "x", [(i, i ^ FAR) for i in range(4)])
    place = jnp.stack([lax.axis_index(name) for name in ("z_hi", "x", "core")]).astype(jnp.int32)
    chunks_shape = shape((parts, 16, 128), jnp.bfloat16)
    over_both = lax.ppermute(over_z, "core", swap)
    behind, over_z = lax.optimization_barrier((products, over_z))
    begun = pl.pallas_call(
        own_tile_kernel,
        out_shape=chunks_shape,
        in_specs=[SMEM] + [VMEM] * 2,
        out_specs=VMEM,
        compiler_params=pltpu.CompilerParams(vmem_limit_bytes=16 << 20),
        cost_estimate=pl.CostEstimate(flops=2 << 23, bytes_accessed=1 << 20, transcendentals=0),
        name="own_tile",
    )(place, pair, behind)
    chunks = pl.pallas_call(
        tile_kernel,
        out_shape=chunks_shape,
        in_specs=[SMEM] + [VMEM] * 7,
        out_specs=VMEM,
        input_output_aliases={7: 0},
        compiler_params=pltpu.CompilerParams(vmem_limit_bytes=16 << 20),
        name="tile",
    )(place, pair, other_pair, products, over_core, over_z, over_both, begun)
    shares = lax.all_to_all(chunks, mesh_axes, 0, 0, tiled=True)
    block = pl.pallas_call(
        sum_kernel,
        out_shape=shape((32, WIDTH), jnp.float32),
        in_specs=[VMEM],
        out_specs=VMEM,
        compiler_params=pltpu.CompilerParams(vmem_limit_bytes=8 << 20),
        name="sum",
    )(shares)
    route = []
    for place in range(512):
        z2, a, c2, h, z, b, c = (int(i) for i in np.unravel_index(place, (2, 4, 2, 2, 2, 4, 2)))
        source = (z2 * 16 + a * 4 + c2 * 2 + h) * 16 + z * 8 + b * 2 + c
        target = (z2 * 16 + b * 4 + c2 * 2 + h) * 16 + z * 8 + a * 2 + c
        route.append((source, target))
    return lax.ppermute(block, whole, route).T


def solution(mesh):
    fine = Mesh(mesh.devices.reshape(8, 4, 2, 4, 2), ("y", "z_lo", "z_hi", "x", "core"))
    over_mesh, over_panel = ("y", "z_lo"), ("z_hi", "x", "core")
    placed = (
        P(over_mesh, over_panel, None),
        P(over_mesh, None, None),
        P(over_mesh),
        P(over_mesh),
        P(over_mesh),
        P(over_mesh),
        P(over_mesh),
    )
    return jax.shard_map(
        local, mesh=fine, in_specs=placed, out_specs=P(over_panel, over_mesh), check_vma=False
    )
```
